32 devices in a mesh: pipe: 2 (over core), tensor: 4 (over y, x), dp: 4 (over z).
Axes of the slice: x: 2, y: 2, z: 4, core: 2. Of those that a mesh axis runs over, the one named last changes fastest.
Arguments:
- ends: bfloat16 [2, 8, 1536, 1024], P('pipe', 'dp', 'tensor'), may hold values from -6 to 6
- segments: int32 [8, 1536], P('dp'), may hold values from 0 to 5, never falling along the last dimension, each value on 1 to 1024 neighbouring positions
- ln_gain: bfloat16 [2, 2, 1024], P('pipe'), may hold values from 0.5 to 1.5
- ln_bias: bfloat16 [2, 2, 1024], P('pipe'), may hold values from -2 to 2
- w_qkv: bfloat16 [2, 1024, 3072], P('pipe', None, 'tensor'), may hold values from -0.1875 to 0.1875
- b_qkv: bfloat16 [2, 3072], P('pipe', 'tensor'), may hold values from -2 to 2
- w_out: bfloat16 [2, 1024, 1024], P('pipe', 'tensor'), may hold values from -1 to 1
- w_in: bfloat16 [2, 1024, 4096], P('pipe', None, 'tensor'), may hold values from -0.1875 to 0.1875
- b_in: bfloat16 [2, 4096], P('pipe', 'tensor'), may hold values from -3 to 3
- w_fc2: bfloat16 [2, 4096, 1024], P('pipe', 'tensor'), may hold values from -0.09375 to 0.09375
- out_bias: bfloat16 [2, 2, 1024], P('pipe'), may hold values from -2 to 2
Outputs:
- boundary: bfloat16 [2, 8, 1536, 1024], P('pipe', 'dp', 'tensor')
- g_ln_gain: float32 [2, 2, 1024], P('pipe', None, ('tensor', 'dp'))
- g_ln_bias: float32 [2, 2, 1024], P('pipe', None, ('tensor', 'dp'))
- g_w_qkv: float32 [2, 1024, 3072], P('pipe', 'dp', 'tensor')
- g_b_qkv: float32 [2, 3072], P('pipe', ('tensor', 'dp'))
- g_w_out: float32 [2, 1024, 1024], P('pipe', ('tensor', 'dp'))
- g_w_in: float32 [2, 1024, 4096], P('pipe', 'dp', 'tensor')
- g_b_in: float32 [2, 4096], P('pipe', ('tensor', 'dp'))
- g_w_fc2: float32 [2, 4096, 1024], P('pipe', ('tensor', 'dp'))
- g_out_bias: float32 [2, 2, 1024], P('pipe', None, ('tensor', 'dp'))
The draws below stay inside these ranges and needn't reach their ends.
Inputs may be any that keep to these rules, and one draw needn't show every extreme that they name: `segments`: each micro-batch of 1536 slots holds 6 whole documents in order, numbered from 0, each of 1 to 1024 tokens, one of exactly 1024.
All inputs are finite; a program needn't handle non-finite values.
Results may differ from the reference program's by a relative error of at most 0.014.
Values may be sent and summed in bfloat16 or wider, within the bound.
No kernel may reach another device: no remote copies, remote signals or barrier semaphores. Data moves between devices by JAX's collectives and lax.ppermute only.
A program may use at most 256 MiB of HBM per device.

```python
import math
import jax
import jax.numpy as jnp
import numpy as np
from jax import lax

D = 1024
HEADS = 16
HEAD_DIM = 64
FF = 4096
ROT = 16
SEQ_MAX = 1024
CAP = 1536
NSEG = 6
ROWS = 8


def levels(rng, shape, shards, smallest, high):
    def one(axis_at, parts):
        heights = jax.random.uniform(jax.random.fold_in(jax.random.fold_in(rng, 6), axis_at), (parts,), jnp.float32, smallest / len(shards), high / len(shards))
        return jnp.repeat(jnp.exp(heights), shape[axis_at] // parts).reshape((-1,) + (1,) * (len(shape) - axis_at - 1))

    level = one(*shards[0])
    for cut in shards[1:]:
        level = level * one(*cut)
    return level


def profile(count, total, reach, lean):
    portions = [(1 << 20) // math.isqrt(rank ** lean) + 1 for rank in range(2, count + 1)]
    surplus, holding = total - reach - (count - 1), [1] * (count - 1)
    while surplus > 0:
        candidates = [i for i in range(count - 1) if holding[i] < reach]
        whole, remaining = sum([portions[i] for i in candidates]), surplus
        for i in candidates:
            addition = min(reach - holding[i], max(1, remaining * portions[i] // whole), surplus)
            holding[i] = holding[i] + addition
            surplus = surplus - addition
    return np.array([reach] + holding)


def uneven_parts(key, amount, total, reach, lean):
    if amount == 2:
        one = jax.random.randint(key, (), max(1, total - reach), min(reach, total - 1) + 1)
        return jnp.stack([one, total - one])
    sizes = jnp.asarray(profile(amount, total, reach, lean), jnp.int32)
    pairs = (amount - 1) // 2
    source_of, receiver = sizes[1:1 + 2 * pairs:2], sizes[2:2 + 2 * pairs:2]
    margin = jnp.minimum(source_of - 1, reach - receiver)
    passed = jax.random.randint(jax.random.fold_in(key, 1), (pairs,), 0, 1 << 20) % (margin + 1)
    sizes = sizes.at[1:1 + 2 * pairs:2].set(source_of - passed).at[2:2 + 2 * pairs:2].set(receiver + passed)
    return sizes[jax.random.permutation(jax.random.fold_in(key, 2), amount)]


def gaussian(stream_key, extent, deviation, bound, split=(), kind=jnp.bfloat16):
    loudness = levels(stream_key, extent, split, -0.22, 0.18) if split else 1.0
    drawn = jax.random.normal(stream_key, extent, jnp.float32) * deviation * loudness
    return jnp.minimum(jnp.maximum(drawn, -bound), bound).astype(kind)


def setup_inputs(seed: int = 0) -> dict:
    streams_of = jax.random.split(jax.random.key(seed), 12)
    return {
        "ends": gaussian(streams_of[0], (2, ROWS, CAP, D), 1.0, 6.0, ((0, 2), (1, 4), (2, 4))),
        "segments": jax.vmap(lambda own: jnp.searchsorted(jnp.cumsum(uneven_parts(own, NSEG, CAP, SEQ_MAX, 2)), jnp.arange(CAP), side="right"))(jax.random.split(streams_of[1], ROWS)).reshape((ROWS, CAP)).astype(jnp.int32),
        "ln_gain": jnp.clip(1.0 + 0.1 * jax.random.normal(streams_of[2], (2, 2, D), jnp.float32), 0.5, 1.5).astype(jnp.bfloat16),
        "ln_bias": gaussian(streams_of[3], (2, 2, D), 0.3, 2.0, ((0, 2),)),
        "w_qkv": gaussian(streams_of[4], (2, D, 3 * D), D ** -0.5, 0.1875, ((0, 2), (2, 4))),
        "b_qkv": gaussian(streams_of[5], (2, 3 * D), 0.3, 2.0, ((0, 2), (1, 4))),
        "w_out": gaussian(streams_of[6], (2, D, D), (D // 32) ** -0.5, 1.0, ((0, 2), (1, 4))),
        "w_in": gaussian(streams_of[7], (2, D, FF), D ** -0.5, 0.1875, ((0, 2), (2, 4))),
        "b_in": gaussian(streams_of[8], (2, FF), 0.5, 3.0, ((0, 2), (1, 4))),
        "w_fc2": gaussian(streams_of[9], (2, FF, D), FF ** -0.5, 0.09375, ((0, 2), (1, 4))),
        "out_bias": gaussian(streams_of[10], (2, 2, D), 0.3, 2.0, ((0, 2),)),
    }


EPSILON = 1e-05
MASKED = -1e+30

@jax.custom_vjp
def low(v):
    return lax.optimization_barrier(v.astype(jnp.bfloat16)).astype(jnp.float32)

@jax.custom_vjp
def low_back(v):
    return v

def low_keep(v):
    return (low(v), None)

def low_pass(kept, grad):
    return (grad,)

def back_keep(v):
    return (v, None)

def back_low(kept, grad):
    return (low(grad),)
low.defvjp(low_keep, low_pass)
low_back.defvjp(back_keep, back_low)

def positions_of(segment_row):
    length = segment_row.shape[0]
    places = jnp.arange(length, dtype=jnp.int32)
    begins = jnp.concatenate([jnp.ones((1,), dtype=jnp.bool_), segment_row[1:] != segment_row[:-1]])
    starts = lax.cummax(jnp.where(begins, places, 0).astype(jnp.int32), axis=0)
    return places - starts

def rotary_tables(positions):
    half_rot = ROT // 2
    frequency = jnp.power(10000.0, -2.0 * jnp.arange(half_rot, dtype=jnp.float32) / ROT)
    angles = positions.astype(jnp.float32)[:, None] * frequency[None, :]
    return (jnp.cos(angles)[:, None, :], jnp.sin(angles)[:, None, :])

def rotate(values, cosine_table, sine_table, direction):
    half_rot = ROT // 2
    front = values[..., :half_rot]
    second = values[..., half_rot:ROT]
    new_front = front * cosine_table - direction * second * sine_table
    new_second = second * cosine_table + direction * front * sine_table
    return jnp.concatenate([new_front, new_second, values[..., ROT:]], axis=-1)

def normalize(inputs):
    centre = lax.optimization_barrier(jnp.mean(inputs, axis=-1, keepdims=True))
    shifted = inputs - centre
    inverse_std = lax.rsqrt(lax.optimization_barrier(jnp.mean(shifted * shifted, axis=-1, keepdims=True)) + EPSILON)
    return (shifted * inverse_std, inverse_std)

def layer(inputs, segment_row, weights, which):
    gains, biases, qkv_weight, qkv_bias, out_weight, in_weight, in_bias, fc2_weight, out_biases = [member[which] for member in weights]
    highest = lax.Precision.HIGHEST
    length = inputs.shape[0]
    cosine_table, sine_table = rotary_tables(positions_of(segment_row))
    normal_rows, inverse_std = normalize(inputs)
    normed_one = low(normal_rows * gains[0] + biases[0])
    normed_two = low(normal_rows * gains[1] + biases[1])
    projected = low_back(jnp.dot(normed_one, qkv_weight, precision=highest) + qkv_bias)
    projected = projected.reshape(length, HEADS, 3, HEAD_DIM)
    queries = low(rotate(projected[:, :, 0], cosine_table, sine_table, 1.0))
    keys_rot = low(rotate(projected[:, :, 1], cosine_table, sine_table, 1.0))
    values = low(projected[:, :, 2])
    factor = 1.0 / math.sqrt(HEAD_DIM)
    raw_scores = low_back(jnp.einsum('qhd,khd->hqk', queries, keys_rot, precision=highest) * factor)
    places = jnp.arange(length, dtype=jnp.int32)
    allowed = jnp.logical_and(places[None, :] <= places[:, None], segment_row[None, :] == segment_row[:, None])
    scores = jnp.where(allowed[None], raw_scores, MASKED)
    top_score = lax.optimization_barrier(jnp.max(scores, axis=-1, keepdims=True))
    exp_scores = jnp.exp(scores - top_score)
    attention_weights = low(exp_scores / lax.optimization_barrier(jnp.sum(exp_scores, axis=-1, keepdims=True)))
    mixed = jnp.einsum('hqk,khd->qhd', attention_weights, values, precision=highest).reshape(length, HEADS * HEAD_DIM)
    mixed = low(low_back(mixed))
    hidden_pre = low_back(jnp.dot(normed_two, in_weight, precision=highest) + in_bias)
    activated = low(jax.nn.gelu(hidden_pre, approximate=False))
    branches = jnp.dot(mixed, out_weight, precision=highest) + jnp.dot(activated, fc2_weight, precision=highest)
    return inputs + branches + out_biases[0] + out_biases[1]

def reference(ends, segments, ln_gain, ln_bias, w_qkv, b_qkv, w_out, w_in, b_in, w_fc2, out_bias):
    weights = tuple((member.astype(jnp.float32) for member in (ln_gain, ln_bias, w_qkv, b_qkv, w_out, w_in, b_in, w_fc2, out_bias)))
    inputs = ends[0].astype(jnp.float32)
    cotangents = ends[1].astype(jnp.float32)

    def one_row(totals, item):
        input_rows, grad_rows, segment_row = item

        def whole_block(block_input, block_weights):
            first_out = layer(block_input, segment_row, block_weights, 0)
            return layer(low(low_back(first_out)), segment_row, block_weights, 1)
        result, pull_back = jax.vjp(whole_block, input_rows, weights)
        input_grad, weight_grads = pull_back(grad_rows)
        totals = tuple((older + newer for older, newer in zip(totals, weight_grads)))
        return (totals, (result.astype(jnp.bfloat16), input_grad.astype(jnp.bfloat16)))
    zeros = tuple((jnp.zeros_like(member) for member in weights))
    totals, (result_rows, grad_rows_all) = lax.scan(one_row, zeros, (inputs, cotangents, segments))
    boundary = jnp.stack([grad_rows_all, result_rows])
    gain_grad, bias_grad, qkv_grad, qkv_bias_grad, out_grad, in_grad, in_bias_grad, fc2_grad, out_bias_grad = totals
    return (boundary, gain_grad, bias_grad, qkv_grad, qkv_bias_grad, out_grad, in_grad, in_bias_grad, fc2_grad, out_bias_grad)
```

```python
import functools
import math

import jax
import jax.numpy as jnp
from jax import lax
from jax.experimental import pallas as pl
from jax.experimental.pallas import tpu as pltpu
from jax.sharding import PartitionSpec as P

HEAD_DIM = 64
ROT = 16
EPSILON = 1e-05
MASKED = -1e30
TILE = 256
SUB = 128
LANES = 128
BF = jnp.bfloat16
F32 = jnp.float32

VM = pltpu.VMEM
NT = (((1,), (1,)), ((), ()))
TN = (((0,), (0,)), ((), ()))


def dot_nn(a, b):
    return jnp.dot(a, b, preferred_element_type=F32)


def dot_nt(a, b):
    return lax.dot_general(a, b, NT, preferred_element_type=F32)


def dot_tn(a, b):
    return lax.dot_general(a, b, TN, preferred_element_type=F32)


def whole(shape):
    return pl.BlockSpec(shape, lambda *_: (0,) * len(shape))


SMEM_SPEC = pl.BlockSpec(memory_space=pltpu.SMEM)
ANY_SPEC = pl.BlockSpec(memory_space=pl.ANY)
PARAMS = pltpu.CompilerParams(vmem_limit_bytes=56 * 1024 * 1024)


def norm_rows(rows):
    centre = jnp.mean(rows, axis=-1, keepdims=True)
    shifted = rows - centre
    inverse_std = lax.rsqrt(jnp.mean(shifted * shifted, axis=-1, keepdims=True) + EPSILON)
    return shifted * inverse_std, inverse_std


def turn(values, tables, direction):
    cos_t, sin_a, sin_b = tables
    width = values.shape[-1]
    times = width // LANES
    wide = lambda t: jnp.concatenate([t] * times, axis=1)
    ahead = pltpu.roll(values, width - ROT // 2, 1)
    behind = pltpu.roll(values, ROT // 2, 1)
    return values * wide(cos_t) + direction * (ahead * wide(sin_a) + behind * wide(sin_b))


def pre_kernel(n_alias, x_ref, gain_ref, bias_ref, wqkv_ref, bqkv_ref, win_ref, bin_ref,
               cos_ref, sa_ref, sb_ref, *rest):
    n1_ref, n2_ref, q_ref, k_ref, v_ref, g_ref, slope_ref, n2_keep = rest[n_alias:]

    @pl.when(pl.program_id(0) == 0)
    def _():
        normal, _ = norm_rows(x_ref[...].astype(F32))
        gains = gain_ref[...].astype(F32)
        biases = bias_ref[...].astype(F32)
        n1 = (normal * gains[0:1] + biases[0:1]).astype(BF)
        n2 = (normal * gains[1:2] + biases[1:2]).astype(BF)
        n1_ref[0] = n1
        n2_ref[0] = n2
        n2_keep[...] = n2
        tables = (cos_ref[...], sa_ref[...], sb_ref[...])
        wide = q_ref.shape[-1]
        scale = 1.0 / math.sqrt(HEAD_DIM)
        bq = bqkv_ref[...].astype(F32)
        part = lambda i: dot_nn(n1, wqkv_ref[:, i * wide:(i + 1) * wide]) + bq[:, i * wide:(i + 1) * wide]
        q_ref[0] = (turn(part(0), tables, 1.0).astype(BF).astype(F32) * scale).astype(BF)
        k_ref[0] = turn(part(1), tables, 1.0).astype(BF)
        v_ref[0] = part(2).astype(BF)

    f = dot_nn(n2_keep[...], win_ref[...]) + bin_ref[...].astype(F32)
    phi = 0.5 * (1.0 + lax.erf(f * (1.0 / math.sqrt(2.0))))
    density = jnp.exp(-0.5 * f * f) * (1.0 / math.sqrt(2.0 * math.pi))
    g_ref[0] = (f * phi).astype(BF)
    slope_ref[0] = (phi + f * density).astype(BF)


def slot_call(kernel, slot, args, in_specs, outs, kept, grid, scratch):
    n_alias = 0 if kept is None else len(outs)
    specs = list(in_specs)
    operands = list(args)
    aliases = {}
    if kept is not None:
        for i, buf in enumerate(kept):
            aliases[len(operands)] = i
            operands.append(buf)
            specs.append(ANY_SPEC)
    return pl.pallas_call(
        functools.partial(kernel, n_alias),
        grid=grid,
        in_specs=specs,
        out_specs=[pl.BlockSpec(block, index) for _, _, block, index in outs],
        out_shape=[jax.ShapeDtypeStruct(shape, dtype) for shape, dtype, _, _ in outs],
        input_output_aliases=aliases,
        scratch_shapes=scratch,
        compiler_params=PARAMS,
    )(*operands)


def pre_slot(slot, slots, x, lp, tables, kept):
    rows, d = x.shape
    wide = lp["w_qkv"].shape[1]
    units = lp["w_in"].shape[1]
    cols = wide // 3
    ck = min(TILE, units)
    first = lambda j: (slot, 0, 0)
    moving = lambda j: (slot, 0, j)
    outs = [((slots, rows, d), BF, (1, rows, d), first)] * 2
    outs += [((slots, rows, cols), BF, (1, rows, cols), first)] * 3
    outs += [((slots, rows, units), BF, (1, rows, ck), moving)] * 2
    in_specs = [whole((rows, d)), whole((2, d)), whole((2, d)), whole((d, wide)), whole((1, wide)),
                pl.BlockSpec((d, ck), lambda j: (0, j)), pl.BlockSpec((1, ck), lambda j: (0, j))]
    in_specs += [pl.BlockSpec((None, rows, LANES), first)] * 3
    args = [x, lp["ln_gain"], lp["ln_bias"], lp["w_qkv"], lp["b_qkv"], lp["w_in"], lp["b_in"], *tables]
    return slot_call(pre_kernel, slot, args, in_specs, outs, kept, (units // ck,), [VM((rows, d), BF)])


def post_kernel(half, o_ref, g_ref, wout_ref, wfc_ref, *rest):
    out_ref = rest[-1]
    part = dot_nn(o_ref[...], wout_ref[...]) + dot_nn(g_ref[...], wfc_ref[...])
    out_ref[...] = part.astype(out_ref.dtype)
    if half is not None:
        rows = rest[0].shape[0]
        at = half * rows
        summed = part[at:at + rows] + rest[0][...].astype(F32)
        out_ref[at:at + rows, :] = summed.astype(out_ref.dtype)


def post_slot(slot, o_all, g_all, lp, half, addend, dtype):
    _, rows, cols = o_all.shape
    units, d = lp["w_fc2"].shape
    ck = min(TILE, d)
    fixed = lambda j: (slot, 0, 0)
    in_specs = [pl.BlockSpec((None, rows, cols), fixed), pl.BlockSpec((None, rows, units), fixed),
                pl.BlockSpec((cols, ck), lambda j: (0, j)), pl.BlockSpec((units, ck), lambda j: (0, j))]
    args = [o_all, g_all, lp["w_out"], lp["w_fc2"]]
    if half is not None:
        in_specs.append(pl.BlockSpec((rows // 2, ck), lambda j: (0, j)))
        args.append(addend)
    return pl.pallas_call(
        functools.partial(post_kernel, half),
        grid=(d // ck,),
        in_specs=in_specs,
        out_specs=pl.BlockSpec((rows, ck), lambda j: (0, j)),
        out_shape=jax.ShapeDtypeStruct((rows, d), dtype),
        compiler_params=PARAMS,
    )(*args)


def bpre_kernel(n_alias, e_ref, wout_ref, wfc_ref, slope_ref, *rest):
    eall_ref, do_ref, df_ref, sums_ref = rest[n_alias:]

    @pl.when(pl.program_id(0) == 0)
    def _():
        eall_ref[0] = e_ref[...]
        do_ref[0] = dot_nt(e_ref[...], wout_ref[...]).astype(BF)

    df = (dot_nt(e_ref[...], wfc_ref[...]) * slope_ref[...].astype(F32)).astype(BF)
    df_ref[0] = df
    sums_ref[0] = jnp.sum(df.astype(F32), axis=0, keepdims=True)


def bpre_slot(slot, slots, e, slope_all, lp, kept):
    rows, d = e.shape
    cols = lp["w_out"].shape[0]
    units = lp["w_fc2"].shape[0]
    ck = min(TILE, units)
    first = lambda j: (slot, 0, 0)
    moving = lambda j: (slot, 0, j)
    outs = [((slots, rows, d), BF, (1, rows, d), first), ((slots, rows, cols), BF, (1, rows, cols), first),
            ((slots, rows, units), BF, (1, rows, ck), moving), ((slots, 1, units), F32, (1, 1, ck), moving)]
    in_specs = [whole((rows, d)), whole((cols, d)), pl.BlockSpec((ck, d), lambda j: (j, 0)),
                pl.BlockSpec((None, rows, ck), moving)]
    args = [e, lp["w_out"], lp["w_fc2"], slope_all]
    return slot_call(bpre_kernel, slot, args, in_specs, outs, kept, (units // ck,), [])


def bpost_kernel(half, ck, x_ref, gain_ref, dqkv_ref, df_ref, wqkv_ref, win_ref, *rest):
    out_ref, sums_ref, normal_keep = rest[-3:]
    j = pl.program_id(0)

    @pl.when(j == 0)
    def _():
        normal, _ = norm_rows(x_ref[...].astype(F32))
        for c in range(normal_keep.shape[0]):
            normal_keep[c] = normal[:, c * ck:(c + 1) * ck]

    one = dot_nt(dqkv_ref[...], wqkv_ref[...])
    two = dot_nt(df_ref[...], win_ref[...])
    normal = normal_keep[j]
    total = lambda v: jnp.sum(v, axis=0, keepdims=True)
    sums_ref[0:1, :] = total(one * normal)
    sums_ref[1:2, :] = total(two * normal)
    sums_ref[2:3, :] = total(one)
    sums_ref[3:4, :] = total(two)
    gains = gain_ref[...].astype(F32)
    part = one * gains[0:1] + two * gains[1:2]
    out_ref[...] = part.astype(out_ref.dtype)
    if half is not None:
        rows = rest[0].shape[0]
        at = half * rows
        summed = part[at:at + rows] + rest[0][...].astype(F32)
        out_ref[at:at + rows, :] = summed.astype(out_ref.dtype)


def bpost_slot(slot, x, dqkv_all, df_all, lp, half, addend, dtype):
    rows, d = x.shape
    wide = dqkv_all.shape[-1]
    units = df_all.shape[-1]
    ck = min(TILE, d)
    fixed = lambda j: (slot, 0, 0)
    in_specs = [whole((rows, d)), pl.BlockSpec((2, ck), lambda j: (0, j)),
                pl.BlockSpec((None, rows, wide), fixed), pl.BlockSpec((None, rows, units), fixed),
                pl.BlockSpec((ck, wide), lambda j: (j, 0)), pl.BlockSpec((ck, units), lambda j: (j, 0))]
    args = [x, lp["ln_gain"], dqkv_all, df_all, lp["w_qkv"], lp["w_in"]]
    if half is not None:
        in_specs.append(pl.BlockSpec((rows // 2, ck), lambda j: (0, j)))
        args.append(addend)
    return pl.pallas_call(
        functools.partial(bpost_kernel, half, ck),
        grid=(d // ck,),
        in_specs=in_specs,
        out_specs=[pl.BlockSpec((rows, ck), lambda j: (0, j)), pl.BlockSpec((4, ck), lambda j: (0, j))],
        out_shape=[jax.ShapeDtypeStruct((rows, d), dtype), jax.ShapeDtypeStruct((4, d), F32)],
        scratch_shapes=[VM((d // ck, rows, ck), F32)],
        compiler_params=PARAMS,
    )(*args)


def head_lanes(shape):
    return lax.broadcasted_iota(jnp.int32, shape, len(shape) - 1) // HEAD_DIM


def by_head(columns, shape):
    group = head_lanes(shape)
    out = jnp.broadcast_to(columns[0], shape)
    for h in range(1, len(columns)):
        out = jnp.where(group == h, columns[h], out)
    return out


def attend_kernel(order_ref, low_ref, q_ref, k_ref, v_ref, start_ref, o_ref, lse_ref,
                  k_abs, v_abs, acc, top, tot):
    subs, _, cols = q_ref.shape
    heads = cols // HEAD_DIM
    per = TILE // SUB
    for i in range(subs):
        src = order_ref[i]
        k_abs[i * SUB:(i + 1) * SUB, :] = k_ref[src]
        v = v_ref[src]
        for h in range(heads):
            v_abs[h, i * SUB:(i + 1) * SUB, :] = jnp.where(head_lanes(v.shape) == h, v, jnp.zeros_like(v))

    def one_query(qb, _):
        q = jnp.concatenate([q_ref[order_ref[qb * per + u]] for u in range(per)], axis=0)
        base = pl.multiple_of(qb * TILE, TILE)
        starts = start_ref[pl.ds(base, TILE), 0:1]
        places = base + lax.broadcasted_iota(jnp.int32, (TILE, 1), 0)
        group = head_lanes(q.shape)
        qs = [jnp.where(group == h, q, jnp.zeros_like(q)) for h in range(heads)]
        lane = lax.broadcasted_iota(jnp.int32, (TILE, TILE), 1)

        def scores(kb):
            at = pl.multiple_of(kb * TILE, TILE)
            keys = k_abs[pl.ds(at, TILE), :]
            allowed = jnp.logical_and(lane + at >= starts, lane + at <= places)
            return at, [jnp.where(allowed, dot_nt(qs[h], keys), MASKED) for h in range(heads)]

        at, found = scores(qb)
        mixed = None
        for h in range(heads):
            m = jnp.max(found[h], axis=1, keepdims=True)
            p = jnp.exp(found[h] - m)
            top[h] = m
            tot[h] = jnp.sum(p, axis=1, keepdims=True)
            pv = dot_nn(p.astype(BF), v_abs[h, pl.ds(at, TILE), :])
            mixed = pv if mixed is None else mixed + pv
        acc[...] = mixed

        def one_key(kb, _):
            at, found = scores(kb)
            fades = []
            mixed = None
            for h in range(heads):
                old = top[h]
                m = jnp.maximum(old, jnp.max(found[h], axis=1, keepdims=True))
                fade = jnp.exp(old - m)
                p = jnp.exp(found[h] - m)
                top[h] = m
                tot[h] = tot[h] * fade + jnp.sum(p, axis=1, keepdims=True)
                pv = dot_nn(p.astype(BF), v_abs[h, pl.ds(at, TILE), :])
                mixed = pv if mixed is None else mixed + pv
                fades.append(fade)
            acc[...] = acc[...] * by_head(fades, (TILE, cols)) + mixed
            return 0

        lax.fori_loop(low_ref[qb], qb, one_key, 0)
        out = (acc[...] / by_head([tot[h] for h in range(heads)], (TILE, cols))).astype(BF)
        for u in range(per):
            o_ref[order_ref[qb * per + u]] = out[u * SUB:(u + 1) * SUB]
        which = lax.broadcasted_iota(jnp.int32, (TILE, LANES), 1)
        logs = jnp.zeros((TILE, LANES), F32)
        for h in range(heads):
            logs = jnp.where(which == h, top[h] + jnp.log(tot[h]), logs)
        lse_ref[pl.ds(base, TILE), :] = logs
        return 0

    lax.fori_loop(0, subs // per, one_query, 0)


def attend(order, low, q, k, v, start_cols):
    subs, _, cols = q.shape
    length = subs * SUB
    heads = cols // HEAD_DIM
    full = [whole(a.shape) for a in (q, k, v, start_cols)]
    return pl.pallas_call(
        attend_kernel,
        grid=(1,),
        in_specs=[SMEM_SPEC, SMEM_SPEC] + full,
        out_specs=[whole(q.shape), whole((length, LANES))],
        out_shape=[jax.ShapeDtypeStruct(q.shape, BF), jax.ShapeDtypeStruct((length, LANES), F32)],
        scratch_shapes=[VM((length, cols), BF), VM((heads, length, cols), BF), VM((TILE, cols), F32),
                        VM((heads, TILE, 1), F32), VM((heads, TILE, 1), F32)],
        compiler_params=PARAMS,
    )(order, low, q, k, v, start_cols)


def attend_back_kernel(order_ref, low_ref, q_ref, k_ref, v_ref, do_ref, o_ref, lse_ref, start_ref,
                       cos_ref, sa_ref, sb_ref, out_ref, sums_ref,
                       k_abs, v_abs, km, dk, dv, dq, qm, dom, stat):
    subs, _, cols = q_ref.shape
    heads = cols // HEAD_DIM
    per = TILE // SUB
    scale = 1.0 / math.sqrt(HEAD_DIM)
    for i in range(subs):
        src = order_ref[i]
        rows = slice(i * SUB, (i + 1) * SUB)
        key = k_ref[src]
        k_abs[rows, :] = key
        v_abs[rows, :] = v_ref[src]
        for h in range(heads):
            km[h, rows, :] = jnp.where(head_lanes(key.shape) == h, key, jnp.zeros_like(key))
        dk[rows, :] = jnp.zeros((SUB, cols), F32)
        dv[rows, :] = jnp.zeros((SUB, cols), F32)
    sums_ref[...] = jnp.zeros(sums_ref.shape, F32)

    def tables(src):
        return cos_ref[src], sa_ref[src], sb_ref[src]

    def emit(src, at, values):
        low = values.astype(BF)
        out_ref[src, :, at:at + cols] = low
        sums_ref[:, at:at + cols] += jnp.sum(low.astype(F32), axis=0, keepdims=True)

    def one_query(qb, _):
        base = pl.multiple_of(qb * TILE, TILE)
        srcs = [order_ref[qb * per + u] for u in range(per)]
        q = jnp.concatenate([q_ref[s] for s in srcs], axis=0)
        do = jnp.concatenate([do_ref[s] for s in srcs], axis=0)
        o = jnp.concatenate([o_ref[s] for s in srcs], axis=0)
        group = head_lanes(q.shape)
        logs = jnp.transpose(lse_ref[pl.ds(base, TILE), :])
        inner = jnp.transpose(do.astype(F32) * o.astype(F32))
        for h in range(heads):
            qm[h] = jnp.where(group == h, q, jnp.zeros_like(q))
            dom[h] = jnp.where(group == h, do, jnp.zeros_like(do))
            stat[h, 0:1, :] = logs[h:h + 1, :]
            stat[h, 1:2, :] = jnp.sum(inner[h * HEAD_DIM:(h + 1) * HEAD_DIM, :], axis=0, keepdims=True)
        dq[...] = jnp.zeros((TILE, cols), F32)
        starts = start_ref[qb]
        places = base + lax.broadcasted_iota(jnp.int32, (1, TILE), 1)
        down = lax.broadcasted_iota(jnp.int32, (TILE, TILE), 0)

        def one_key(kb, _):
            at = pl.multiple_of(kb * TILE, TILE)
            keys = k_abs[pl.ds(at, TILE), :]
            vals = v_abs[pl.ds(at, TILE), :]
            allowed = jnp.logical_and(down + at >= starts, down + at <= places)
            dk_new = dv_new = dq_new = None
            more = lambda old, new: new if old is None else old + new
            for h in range(heads):
                s = dot_nt(keys, qm[h])
                p = jnp.exp(jnp.where(allowed, s - stat[h, 0:1, :], MASKED))
                dp = dot_nt(vals, dom[h])
                ds = (p * (dp - stat[h, 1:2, :])).astype(BF)
                dv_new = more(dv_new, dot_nn(p.astype(BF), dom[h]))
                dk_new = more(dk_new, dot_nn(ds, qm[h]))
                dq_new = more(dq_new, dot_tn(ds, km[h, pl.ds(at, TILE), :]))
            dv[pl.ds(at, TILE), :] += dv_new
            dk[pl.ds(at, TILE), :] += dk_new
            dq[...] += dq_new
            return 0

        lax.fori_loop(low_ref[qb], qb + 1, one_key, 0)
        for u in range(per):
            emit(srcs[u], 0, turn(dq[u * SUB:(u + 1) * SUB, :] * scale, tables(srcs[u]), -1.0))
        return 0

    lax.fori_loop(0, subs // per, one_query, 0)
    for i in range(subs):
        src = order_ref[i]
        rows = slice(i * SUB, (i + 1) * SUB)
        emit(src, cols, turn(dk[rows, :], tables(src), -1.0))
        emit(src, 2 * cols, dv[rows, :])


def attend_back(order, low, q, k, v, do, o, lse, start_rows, tables):
    subs, _, cols = q.shape
    length = subs * SUB
    heads = cols // HEAD_DIM
    args = (q, k, v, do, o, lse, start_rows, *tables)
    return pl.pallas_call(
        attend_back_kernel,
        grid=(1,),
        in_specs=[SMEM_SPEC, SMEM_SPEC] + [whole(a.shape) for a in args],
        out_specs=[whole((subs, SUB, 3 * cols)), whole((1, 3 * cols))],
        out_shape=[jax.ShapeDtypeStruct((subs, SUB, 3 * cols), BF), jax.ShapeDtypeStruct((1, 3 * cols), F32)],
        scratch_shapes=[VM((length, cols), BF), VM((length, cols), BF), VM((heads, length, cols), BF),
                        VM((length, cols), F32), VM((length, cols), F32), VM((TILE, cols), F32),
                        VM((heads, TILE, cols), BF), VM((heads, TILE, cols), BF), VM((heads, 2, TILE), F32)],
        compiler_params=PARAMS,
    )(order, low, *args)


def across(x, k):
    n = lax.axis_size("tensor")
    return lax.ppermute(x, "tensor", [(i, i ^ k) for i in range(n)])


def swap(x):
    return lax.ppermute(x, "pipe", [(0, 1), (1, 0)])


def gather_slots(x):
    half = x.shape[0] // 2
    one = across(x, 1)
    two = across(x, 2)
    far_a = across(one[:half], 2)
    far_b = across(two[half:], 1)
    return [x, one, two, jnp.concatenate([far_a, far_b], axis=0)]


def reduce_slots(make):
    far, *extra3 = make(3, None, None, BF)
    half = far.shape[0] // 2
    from_one = across(far[:half], 1)
    from_two = across(far[half:], 2)
    own, *extra0 = make(0, None, None, F32)
    first, *extra1 = make(1, 1, from_two, BF)
    got_one = across(first, 1)
    second, *extra2 = make(2, 0, from_one, BF)
    got_two = across(second, 2)
    total = own + got_one.astype(F32) + got_two.astype(F32)
    return total, [extra0, extra1, extra2, extra3]


def line_reduce(blocks, axis):
    n = lax.axis_size(axis)
    me = lax.axis_index(axis)
    take = lambda i: lax.dynamic_index_in_dim(blocks, jnp.clip(i, 0, n - 1), 0, keepdims=False)
    right = left = None
    for step in range(1, n):
        reach = n - step
        up, down = take(me + reach), take(me - reach)
        if right is not None:
            up = (up.astype(F32) + right.astype(F32)).astype(blocks.dtype)
            down = (down.astype(F32) + left.astype(F32)).astype(blocks.dtype)
        right = lax.ppermute(up, axis, [(i, i + 1) for i in range(n - 1) if i + reach <= n - 1])
        left = lax.ppermute(down, axis, [(i, i - 1) for i in range(1, n) if i - reach >= 0])
    total = take(me).astype(F32)
    if right is not None:
        total = total + right.astype(F32) + left.astype(F32)
    return total


def spread_reduce(vec, axis):
    n = lax.axis_size(axis)
    me = lax.axis_index(axis)
    total = lax.dynamic_index_in_dim(vec, me, 0, keepdims=False)
    for k in range(1, n):
        block = lax.dynamic_index_in_dim(vec, (me + k) % n, 0, keepdims=False)
        total = total + lax.ppermute(block, axis, [(i, (i + k) % n) for i in range(n)])
    return total


def forward_layer(x, lp, geo):
    slots = gather_slots(x)
    kept = None
    for k in range(len(slots)):
        kept = pre_slot(k, len(slots), slots[k], lp, geo["tables"], kept)
    n1, n2, q, k, v, g, slope = kept
    flat = lambda a: a.reshape(-1, SUB, a.shape[-1])
    o, lse = attend(geo["order"], geo["low"], flat(q), flat(k), flat(v), geo["start_cols"])
    o_slots = o.reshape(q.shape)
    make = lambda slot, half, addend, dtype: (post_slot(slot, o_slots, g, lp, half, addend, dtype),)
    summed, _ = reduce_slots(make)
    out_biases = lp["out_bias"].astype(F32)
    result = x.astype(F32) + summed + out_biases[0] + out_biases[1]
    saved = dict(slots=slots, n1=n1, n2=n2, q=flat(q), k=flat(k), v=flat(v), g=g, slope=slope, o=o, lse=lse)
    return result.astype(BF), saved


def backward_layer(e, lp, saved, geo):
    slots = gather_slots(e)
    kept = None
    for k in range(len(slots)):
        kept = bpre_slot(k, len(slots), slots[k], saved["slope"], lp, kept)
    e_all, do, df, bin_parts = kept
    flat = lambda a: a.reshape(-1, SUB, a.shape[-1])
    tables = [flat(t) for t in geo["tables"]]
    dqkv, bqkv_grad = attend_back(geo["order"], geo["low"], saved["q"], saved["k"], saved["v"], flat(do),
                                  saved["o"], saved["lse"], geo["start_rows"], tables)
    dqkv_slots = dqkv.reshape(len(slots), -1, dqkv.shape[-1])
    make = lambda slot, half, addend, dtype: bpost_slot(
        slot, saved["slots"][slot], dqkv_slots, df, lp, half, addend, dtype)
    u, extras = reduce_slots(make)
    col_sums = sum(item[0] for item in extras)
    x_rows, e_rows = saved["slots"][0].astype(F32), e.astype(F32)
    normal, inverse_std = norm_rows(x_rows)
    mean_grad = jnp.mean(u, axis=-1, keepdims=True)
    mean_cross = jnp.mean(u * normal, axis=-1, keepdims=True)
    dx = e_rows + (u - mean_grad - normal * mean_cross) * inverse_std
    rows2 = lambda a: a.reshape(-1, a.shape[-1])
    wgrad = lambda a, b: dot_tn(rows2(a), rows2(b)).astype(BF)
    grads = dict(
        w_out=wgrad(saved["o"], e_all),
        w_fc2=wgrad(saved["g"], e_all),
        w_in=wgrad(saved["n2"], df),
        w_qkv=wgrad(saved["n1"], dqkv),
    )
    small = jnp.concatenate([col_sums, jnp.sum(e_rows, axis=0, keepdims=True)], axis=0)
    bias_grads = jnp.concatenate([bqkv_grad[0], jnp.sum(bin_parts, axis=(0, 1))])
    return dx.astype(BF), grads, small, bias_grads


NAMES = ("w_qkv", "w_out", "w_in", "w_fc2")


def reduce_weights(grads, is_first):
    out = {}
    n = lax.axis_size("dp")
    for name in NAMES:
        g = grads[name]
        parts = g.reshape(n, 2, g.shape[0] // n // 2, g.shape[1])
        give = jnp.where(is_first, parts[:, 1], parts[:, 0])
        keep = jnp.where(is_first, parts[:, 0], parts[:, 1])
        both = (keep.astype(F32) + swap(give).astype(F32)).astype(BF)
        out[name] = line_reduce(both, "dp").astype(BF)
    return out


def column_order(a, direction):
    shape = a.shape
    heads = shape[-1] // (3 * HEAD_DIM)
    dims = (heads, 3) if direction > 0 else (3, heads)
    split = a.reshape(*shape[:-1], *dims, HEAD_DIM)
    return jnp.swapaxes(split, -2, -3).reshape(shape)


def body(ends, segments, ln_gain, ln_bias, w_qkv, b_qkv, w_out, w_in, b_in, w_fc2, out_bias):
    is_first = lax.axis_index("pipe") == 0
    me = lax.axis_index("tensor")
    n_tensor = lax.axis_size("tensor")
    choose = lambda a, b: jnp.where(is_first, a, b)
    shares = ends[0]
    rows, d = shares.shape[1:]

    keep = choose(shares[0], shares[1])
    got = swap(choose(shares[1], shares[0]))
    x0 = choose(keep, got)
    e1 = choose(got, keep)

    own = dict(ln_gain=ln_gain[0], ln_bias=ln_bias[0], w_qkv=column_order(w_qkv[0], 1),
               b_qkv=column_order(b_qkv, 1), w_out=w_out[0], w_in=w_in[0], b_in=b_in, w_fc2=w_fc2[0],
               out_bias=out_bias[0])
    small_names = ("ln_gain", "ln_bias", "b_qkv", "b_in", "out_bias")
    packed = jnp.concatenate([own[s].reshape(-1) for s in small_names]).reshape(-1, LANES)
    other_packed = swap(packed).reshape(-1)
    other = {name: swap(own[name]) for name in NAMES}
    at = 0
    for s in small_names:
        other[s] = other_packed[at:at + own[s].size].reshape(own[s].shape)
        at += own[s].size
    layer0 = {name: choose(own[name], other[name]) for name in own}
    layer1 = {name: choose(other[name], own[name]) for name in own}

    segment_row = choose(segments[0], segments[1])
    length = segment_row.shape[0]
    places = jnp.arange(length, dtype=jnp.int32)
    begins = jnp.concatenate([jnp.ones((1,), dtype=jnp.bool_), segment_row[1:] != segment_row[:-1]])
    starts = lax.cummax(jnp.where(begins, places, 0), axis=0)
    slot_index = jnp.arange(n_tensor, dtype=jnp.int32) ^ me
    by_slot = jnp.take((places - starts).reshape(n_tensor, rows), slot_index, axis=0)
    lane = jnp.arange(LANES, dtype=jnp.int32) % HEAD_DIM
    half_rot = ROT // 2
    frequency = jnp.power(10000.0, -2.0 * (lane % half_rot).astype(F32) / ROT)
    angles = by_slot.astype(F32)[:, :, None] * frequency
    sines = jnp.sin(angles)
    tables = (jnp.where(lane < ROT, jnp.cos(angles), 1.0),
              jnp.where(lane < half_rot, -sines, 0.0),
              jnp.where(jnp.logical_and(lane >= half_rot, lane < ROT), sines, 0.0))
    per = rows // SUB
    subs = jnp.arange(length // SUB, dtype=jnp.int32)
    geo = dict(
        tables=tables,
        order=(((subs // per) ^ me) * per + subs % per).astype(jnp.int32),
        low=(starts.reshape(-1, TILE)[:, 0] // TILE).astype(jnp.int32),
        start_cols=jnp.broadcast_to(starts[:, None], (length, LANES)),
        start_rows=starts.reshape(-1, 1, TILE),
    )

    h, saved0 = forward_layer(x0, layer0, geo)
    y1, saved1 = forward_layer(h, layer1, geo)
    e0, grads1, small1, bias1 = backward_layer(e1, layer1, saved1, geo)
    half1 = reduce_weights(grads1, is_first)
    dx0, grads0, small0, bias0 = backward_layer(e0, layer0, saved0, geo)
    half0 = reduce_weights(grads0, is_first)

    got = swap(choose(y1, dx0))
    mine = choose(dx0, y1)
    boundary = jnp.stack([choose(mine, got), choose(got, mine)])[None]

    full = {}
    for name in NAMES:
        got = swap(choose(half1[name], half0[name]))
        mine = choose(half0[name], half1[name])
        full[name] = jnp.concatenate([choose(mine, got), choose(got, mine)], axis=0).astype(F32)

    n_dp = lax.axis_size("dp")
    small = choose(small0, small1) + swap(choose(small1, small0))
    bias = choose(bias0, bias1) + swap(choose(bias1, bias0))
    small = jnp.moveaxis(small.reshape(small.shape[0], n_tensor, -1), 1, 0)
    small = spread_reduce(small, "tensor")
    small = jnp.moveaxis(small.reshape(small.shape[0], n_dp, -1), 1, 0)
    n_qkv = b_qkv.size
    bias = jnp.concatenate([bias[:n_qkv].reshape(n_dp, -1), bias[n_qkv:].reshape(n_dp, -1)], axis=1)
    back = column_order(bias_qkv_whole(bias, n_qkv, n_dp), -1).reshape(n_dp, -1)
    bias = jnp.concatenate([back, bias[:, n_qkv // n_dp:]], axis=1)
    line = jnp.concatenate([small.reshape(n_dp, -1), bias], axis=1)
    line = spread_reduce(line, "dp")
    n_small = small.shape[1] * small.shape[2]
    sums = line[:n_small].reshape(small.shape[1:])
    bias = line[n_small:]
    g_b_qkv, g_b_in = bias[:n_qkv // n_dp], bias[n_qkv // n_dp:]
    g_gain, g_bias = sums[None, 0:2], sums[None, 2:4]
    g_out_bias = jnp.stack([sums[4], sums[4]])[None]
    return (
        boundary,
        g_gain,
        g_bias,
        column_order(full["w_qkv"], -1)[None],
        g_b_qkv[None],
        full["w_out"][None],
        full["w_in"][None],
        g_b_in[None],
        full["w_fc2"][None],
        g_out_bias,
    )


def bias_qkv_whole(bias, n_qkv, n_dp):
    return bias[:, :n_qkv // n_dp].reshape(1, n_qkv)


def solution(mesh):
    placed = (
        P("pipe", "dp", "tensor", None),
        P("dp", None),
        P("pipe", None, None),
        P("pipe", None, None),
        P("pipe", None, "tensor"),
        P("pipe", "tensor"),
        P("pipe", "tensor", None),
        P("pipe", None, "tensor"),
        P("pipe", "tensor"),
        P("pipe", "tensor", None),
        P("pipe", None, None),
    )
    return jax.shard_map(
        body,
        mesh=mesh,
        in_specs=placed,
        out_specs=(
            P("pipe", "dp", "tensor", None),
            P("pipe", None, ("tensor", "dp")),
            P("pipe", None, ("tensor", "dp")),
            P("pipe", "dp", "tensor"),
            P("pipe", ("tensor", "dp")),
            P("pipe", ("tensor", "dp"), None),
            P("pipe", "dp", "tensor"),
            P("pipe", ("tensor", "dp")),
            P("pipe", ("tensor", "dp"), None),
            P("pipe", None, ("tensor", "dp")),
        ),
        check_vma=False,
    )
```

```python
import functools
import math

import jax
import jax.numpy as jnp
from jax import lax
from jax.experimental import pallas as pl
from jax.experimental.pallas import tpu as pltpu
from jax.sharding import PartitionSpec as P

HEAD_DIM = 64
ROT = 16
EPSILON = 1e-05
MASKED = -1e30
TILE = 256
CHUNK = 512
SUB = 128
LANES = 128
BF = jnp.bfloat16
F32 = jnp.float32

VM = pltpu.VMEM
NT = (((1,), (1,)), ((), ()))
TN = (((0,), (0,)), ((), ()))


def dot_nn(a, b):
    return jnp.dot(a, b, preferred_element_type=F32)


def dot_nt(a, b):
    return lax.dot_general(a, b, NT, preferred_element_type=F32)


def dot_tn(a, b):
    return lax.dot_general(a, b, TN, preferred_element_type=F32)


def whole(shape):
    return pl.BlockSpec(shape, lambda *_: (0,) * len(shape))


SMEM_SPEC = pl.BlockSpec(memory_space=pltpu.SMEM)
ANY_SPEC = pl.BlockSpec(memory_space=pl.ANY)
PARAMS = pltpu.CompilerParams(vmem_limit_bytes=56 * 1024 * 1024)


def cost(flops, moved):
    return pl.CostEstimate(flops=int(flops), bytes_accessed=int(moved), transcendentals=0)


def norm_rows(rows):
    centre = jnp.mean(rows, axis=-1, keepdims=True)
    shifted = rows - centre
    inverse_std = lax.rsqrt(jnp.mean(shifted * shifted, axis=-1, keepdims=True) + EPSILON)
    return shifted * inverse_std, inverse_std


def turn(values, tables, direction):
    cos_t, sin_a, sin_b = tables
    width = values.shape[-1]
    times = width // LANES
    wide = lambda t: jnp.concatenate([t] * times, axis=1)
    ahead = pltpu.roll(values, width - ROT // 2, 1)
    behind = pltpu.roll(values, ROT // 2, 1)
    return values * wide(cos_t) + direction * (ahead * wide(sin_a) + behind * wide(sin_b))


SLOTS = (1, 2, 0, 3)
OWN, NEAR, FAR, ENDS = (1, 2), (2, 0), (1, 3), (2, 1)


def stacked(refs):
    parts = [r[...] for r in refs]
    return parts[0] if len(parts) == 1 else jnp.concatenate(parts, axis=0)


def pre_kernel(n_x, n_alias, *refs):
    x_refs = refs[:n_x]
    (gain_ref, bias_ref, wqkv_ref, bqkv_ref, win_ref, bin_ref, cos_ref, sa_ref, sb_ref) = refs[n_x:n_x + 9]
    n1_ref, n2_ref, q_ref, k_ref, v_ref, g_ref, slope_ref, n2_keep = refs[n_x + 9 + n_alias:]

    @pl.when(pl.program_id(0) == 0)
    def _():
        normal, _ = norm_rows(stacked(x_refs).astype(F32))
        gains = gain_ref[...].astype(F32)
        biases = bias_ref[...].astype(F32)
        n1 = (normal * gains[0:1] + biases[0:1]).astype(BF)
        n2 = (normal * gains[1:2] + biases[1:2]).astype(BF)
        n1_ref[...] = n1.reshape(n1_ref.shape)
        n2_ref[...] = n2.reshape(n2_ref.shape)
        n2_keep[...] = n2
        flat = lambda r: r[...].reshape(n1.shape[0], LANES)
        tables = (flat(cos_ref), flat(sa_ref), flat(sb_ref))
        wide = q_ref.shape[-1]
        scale = 1.0 / math.sqrt(HEAD_DIM)
        bq = bqkv_ref[...].astype(F32)
        part = lambda i: dot_nn(n1, wqkv_ref[:, i * wide:(i + 1) * wide]) + bq[:, i * wide:(i + 1) * wide]
        q = (turn(part(0), tables, 1.0).astype(BF).astype(F32) * scale).astype(BF)
        q_ref[...] = q.reshape(q_ref.shape)
        k_ref[...] = turn(part(1), tables, 1.0).astype(BF).reshape(k_ref.shape)
        v_ref[...] = part(2).astype(BF).reshape(v_ref.shape)

    f = dot_nn(n2_keep[...], win_ref[...]) + bin_ref[...].astype(F32)
    phi = 0.5 * (1.0 + lax.erf(f * (1.0 / math.sqrt(2.0))))
    density = jnp.exp(-0.5 * f * f) * (1.0 / math.sqrt(2.0 * math.pi))
    g_ref[...] = (f * phi).astype(BF).reshape(g_ref.shape)
    slope_ref[...] = (phi + f * density).astype(BF).reshape(slope_ref.shape)


def group_call(kernel, args, in_specs, outs, kept, grid, scratch, price):
    n_alias = 0 if kept is None else len(outs)
    specs = list(in_specs)
    operands = list(args)
    aliases = {}
    if kept is not None:
        for i, buf in enumerate(kept):
            aliases[len(operands)] = i
            operands.append(buf)
            specs.append(ANY_SPEC)
    return pl.pallas_call(
        functools.partial(kernel, n_alias),
        grid=grid,
        in_specs=specs,
        out_specs=[pl.BlockSpec(block, index) for _, _, block, index in outs],
        out_shape=[jax.ShapeDtypeStruct(shape, dtype) for shape, dtype, _, _ in outs],
        input_output_aliases=aliases,
        scratch_shapes=scratch,
        compiler_params=PARAMS,
        cost_estimate=price,
    )(*operands)


def pre_group(group, xs, lp, tables, kept):
    size, at = group
    d = xs[0].shape[1]
    slots, rows = len(SLOTS), tables[0].shape[1]
    total = size * rows
    wide = lp["w_qkv"].shape[1]
    units = lp["w_in"].shape[1]
    cols = wide // 3
    ck = min(CHUNK, units)
    first = lambda j: (at, 0, 0)
    moving = lambda j: (at, 0, j)
    outs = [((slots, rows, d), BF, (size, rows, d), first)] * 2
    outs += [((slots, rows, cols), BF, (size, rows, cols), first)] * 3
    outs += [((slots, rows, units), BF, (size, rows, ck), moving)] * 2
    in_specs = [whole(x.shape) for x in xs]
    in_specs += [whole((2, d)), whole((2, d)), whole((d, wide)), whole((1, wide)),
                 pl.BlockSpec((d, ck), lambda j: (0, j)), pl.BlockSpec((1, ck), lambda j: (0, j))]
    in_specs += [pl.BlockSpec((size, rows, LANES), first)] * 3
    args = [*xs, lp["ln_gain"], lp["ln_bias"], lp["w_qkv"], lp["b_qkv"], lp["w_in"], lp["b_in"], *tables]
    return group_call(functools.partial(pre_kernel, len(xs)), args, in_specs, outs, kept, (units // ck,),
                      [VM((total, d), BF)],
                      cost(2 * total * d * (wide + units), 2 * d * (wide + units) + 10 * total * d))


def share(part, addend_refs, outs):
    if len(outs) == 3:
        own, far_a, far_b = outs
        rows, half = own.shape[0], far_a.shape[0]
        own[...] = part[:rows]
        far_a[...] = part[rows:rows + half].astype(BF)
        far_b[...] = part[rows + half:].astype(BF)
        return
    one, two = outs
    from_two, from_one = addend_refs
    rows, half = one.shape[0], from_two.shape[0]
    one[:half, :] = part[:half].astype(BF)
    one[half:, :] = (part[half:rows] + from_two[...].astype(F32)).astype(BF)
    two[:half, :] = (part[rows:rows + half] + from_one[...].astype(F32)).astype(BF)
    two[half:, :] = part[rows + half:].astype(BF)


def share_specs(group, rows, d, ck):
    col = lambda j: (0, j)
    if group == ENDS:
        shapes = [((rows, d), F32), ((rows // 2, d), BF), ((rows // 2, d), BF)]
    else:
        shapes = [((rows, d), BF), ((rows, d), BF)]
    return [pl.BlockSpec((s[0], ck), col) for s, _ in shapes], [jax.ShapeDtypeStruct(s, t) for s, t in shapes]


def post_kernel(n_add, o_ref, g_ref, wout_ref, wfc_ref, *rest):
    total = o_ref.shape[0] * o_ref.shape[1]
    o = o_ref[...].reshape(total, o_ref.shape[-1])
    g = g_ref[...].reshape(total, g_ref.shape[-1])
    share(dot_nn(o, wout_ref[...]) + dot_nn(g, wfc_ref[...]), rest[:n_add], rest[n_add:])


def post_group(group, o_all, g_all, lp, addends):
    size, at = group
    _, rows, cols = o_all.shape
    units, d = lp["w_fc2"].shape
    ck = min(CHUNK, d)
    fixed = lambda j: (at, 0, 0)
    in_specs = [pl.BlockSpec((size, rows, cols), fixed), pl.BlockSpec((size, rows, units), fixed),
                pl.BlockSpec((cols, ck), lambda j: (0, j)), pl.BlockSpec((units, ck), lambda j: (0, j))]
    in_specs += [pl.BlockSpec((a.shape[0], ck), lambda j: (0, j)) for a in addends]
    out_specs, out_shape = share_specs(group, rows, d, ck)
    total = size * rows
    return pl.pallas_call(
        functools.partial(post_kernel, len(addends)),
        grid=(d // ck,),
        in_specs=in_specs,
        out_specs=out_specs,
        out_shape=out_shape,
        compiler_params=PARAMS,
        cost_estimate=cost(2 * total * d * (cols + units), 2 * d * (cols + units) + 5 * total * d),
    )(o_all, g_all, lp["w_out"], lp["w_fc2"], *addends)


def bpre_kernel(n_x, n_alias, *refs):
    e_refs = refs[:n_x]
    wout_ref, wfc_ref, slope_ref = refs[n_x:n_x + 3]
    eall_ref, do_ref, df_ref, sums_ref = refs[n_x + 3 + n_alias:]
    e = stacked(e_refs)

    @pl.when(pl.program_id(0) == 0)
    def _():
        eall_ref[...] = e.reshape(eall_ref.shape)
        do_ref[...] = dot_nt(e, wout_ref[...]).astype(BF).reshape(do_ref.shape)

    back = dot_nt(e, wfc_ref[...])
    df = (back * slope_ref[...].reshape(back.shape).astype(F32)).astype(BF)
    df_ref[...] = df.reshape(df_ref.shape)
    sums = jnp.sum(df.astype(F32).reshape(df_ref.shape), axis=1, keepdims=True)
    sums_ref[...] = sums


def bpre_group(group, es, slope_all, lp, kept):
    size, at = group
    d = es[0].shape[1]
    slots, rows, units = slope_all.shape
    cols = lp["w_out"].shape[0]
    ck = min(CHUNK, units)
    first = lambda j: (at, 0, 0)
    moving = lambda j: (at, 0, j)
    outs = [((slots, rows, d), BF, (size, rows, d), first), ((slots, rows, cols), BF, (size, rows, cols), first),
            ((slots, rows, units), BF, (size, rows, ck), moving), ((slots, 1, units), F32, (size, 1, ck), moving)]
    in_specs = [whole(e.shape) for e in es]
    in_specs += [whole((cols, d)), pl.BlockSpec((ck, d), lambda j: (j, 0)),
                 pl.BlockSpec((size, rows, ck), moving)]
    args = [*es, lp["w_out"], lp["w_fc2"], slope_all]
    total = size * rows
    return group_call(functools.partial(bpre_kernel, len(es)), args, in_specs, outs, kept, (units // ck,), [],
                      cost(2 * total * d * (cols + units), 2 * d * (cols + units) + 8 * total * d))


def bpost_kernel(n_x, n_add, ck, *refs):
    x_refs = refs[:n_x]
    gain_ref, dqkv_ref, df_ref, wqkv_ref, win_ref = refs[n_x:n_x + 5]
    addend_refs = refs[n_x + 5:n_x + 5 + n_add]
    outs = refs[n_x + 5 + n_add:-2]
    sums_ref, normal_keep = refs[-2:]
    j = pl.program_id(0)

    @pl.when(j == 0)
    def _():
        normal, _ = norm_rows(stacked(x_refs).astype(F32))
        for c in range(normal_keep.shape[0]):
            normal_keep[c] = normal[:, c * ck:(c + 1) * ck]

    normal = normal_keep[j]
    flat = lambda r: r[...].reshape(normal.shape[0], r.shape[-1])
    one = dot_nt(flat(dqkv_ref), wqkv_ref[...])
    two = dot_nt(flat(df_ref), win_ref[...])
    total = lambda v: jnp.sum(v, axis=0, keepdims=True)
    sums_ref[0:1, :] = total(one * normal)
    sums_ref[1:2, :] = total(two * normal)
    sums_ref[2:3, :] = total(one)
    sums_ref[3:4, :] = total(two)
    gains = gain_ref[...].astype(F32)
    share(one * gains[0:1] + two * gains[1:2], addend_refs, outs)


def bpost_group(group, xs, dqkv_all, df_all, lp, addends):
    size, at = group
    d = xs[0].shape[1]
    _, rows, wide = dqkv_all.shape
    units = df_all.shape[-1]
    ck = min(CHUNK, d)
    total = size * rows
    fixed = lambda j: (at, 0, 0)
    in_specs = [whole(x.shape) for x in xs]
    in_specs += [pl.BlockSpec((2, ck), lambda j: (0, j)),
                 pl.BlockSpec((size, rows, wide), fixed), pl.BlockSpec((size, rows, units), fixed),
                 pl.BlockSpec((ck, wide), lambda j: (j, 0)), pl.BlockSpec((ck, units), lambda j: (j, 0))]
    in_specs += [pl.BlockSpec((a.shape[0], ck), lambda j: (0, j)) for a in addends]
    out_specs, out_shape = share_specs(group, rows, d, ck)
    return pl.pallas_call(
        functools.partial(bpost_kernel, len(xs), len(addends), ck),
        grid=(d // ck,),
        in_specs=in_specs,
        out_specs=out_specs + [pl.BlockSpec((4, ck), lambda j: (0, j))],
        out_shape=out_shape + [jax.ShapeDtypeStruct((4, d), F32)],
        scratch_shapes=[VM((d // ck, total, ck), F32)],
        compiler_params=PARAMS,
        cost_estimate=cost(2 * total * d * (wide + units), 2 * d * (wide + units) + 7 * total * d),
    )(*xs, lp["ln_gain"], dqkv_all, df_all, lp["w_qkv"], lp["w_in"], *addends)


def wgrad_kernel(with_out, core_ref, *refs):
    first = core_ref[0] == 0
    if with_out:
        keep_ref, give_ref, whole_out = refs[-3:]
        pairs = list(refs[2:-3])
    else:
        keep_ref, give_ref = refs[-2:]
        pairs = list(refs[:-2])
    many, half, _ = keep_ref.shape

    def store(b, rows, cols, zero, one):
        keep_ref[b, rows, cols] = jnp.where(first, zero, one).astype(BF)
        give_ref[b, rows, cols] = jnp.where(first, one, zero).astype(BF)

    at = 0
    if with_out:
        o_ref, e_ref = refs[:2]
        cols = o_ref.shape[1]
        j = pl.program_id(0)

        @pl.when(j == 0)
        def _():
            whole_out[...] = dot_tn(o_ref[...], e_ref[...])

        groups = e_ref.shape[1] // cols
        few = half // groups
        for b in range(many):
            start = 2 * (j * many + b)
            zero, one = [whole_out[pl.ds(pl.multiple_of((start + h) * few, few), few), :] for h in range(2)]
            for c in range(groups):
                part = slice(c * cols, (c + 1) * cols)
                store(b, slice(c * few, (c + 1) * few), slice(0, cols), zero[:, part], one[:, part])
        at = cols
        pairs.append(e_ref)
    for a_ref, b_ref in zip(pairs[0::2], pairs[1::2]):
        wide = b_ref.shape[1]
        product = dot_tn(a_ref[...], b_ref[...])
        for b in range(many):
            low = 2 * b * half
            store(b, slice(None), slice(at, at + wide), product[low:low + half], product[low + half:low + 2 * half])
        at += wide


def wgrad_shapes(d, cols):
    n = lax.axis_size("dp")
    block = d // n
    lanes = max(block, LANES)
    many = lanes // block
    specs = [pl.BlockSpec((many, block // 2, cols), lambda j: (j, 0, 0))] * 2
    shapes = [jax.ShapeDtypeStruct((n, block // 2, cols), BF)] * 2
    return d // lanes, lanes, specs, shapes


def wgrad_early(core, o, e, n2, df, g):
    length, d = e.shape
    cols = o.shape[1] + df.shape[1] + d
    steps, lanes, specs, shapes = wgrad_shapes(d, cols)
    moving = pl.BlockSpec((length, lanes), lambda j: (0, j))
    return pl.pallas_call(
        functools.partial(wgrad_kernel, True),
        grid=(steps,),
        in_specs=[SMEM_SPEC, whole(o.shape), whole(e.shape), moving, whole(df.shape), moving],
        out_specs=specs,
        out_shape=shapes,
        scratch_shapes=[VM((o.shape[1], d), F32)],
        compiler_params=PARAMS,
        cost_estimate=cost(2 * length * d * cols, 2 * length * 4 * d + 2 * d * cols),
    )(core, o, e, n2, df, g)


def wgrad_late(core, n1, dqkv):
    length, d = n1.shape
    cols = dqkv.shape[1]
    steps, lanes, specs, shapes = wgrad_shapes(d, cols)
    return pl.pallas_call(
        functools.partial(wgrad_kernel, False),
        grid=(steps,),
        in_specs=[SMEM_SPEC, pl.BlockSpec((length, lanes), lambda j: (0, j)), whole(dqkv.shape)],
        out_specs=specs,
        out_shape=shapes,
        compiler_params=PARAMS,
        cost_estimate=cost(2 * length * d * cols, 2 * length * 2 * d + 2 * d * cols),
    )(core, n1, dqkv)


def head_lanes(shape):
    return lax.broadcasted_iota(jnp.int32, shape, len(shape) - 1) // HEAD_DIM


def attend_kernel(order_ref, low_ref, q_ref, k_ref, v_ref, start_ref, o_ref, lse_ref,
                  k_abs, v_turned, acc, qm, top, tot):
    subs, _, cols = q_ref.shape
    heads = cols // HEAD_DIM
    per = TILE // SUB
    blocks = subs // per
    for b in range(blocks):
        pair = [order_ref[b * per + u] for u in range(per)]
        k_abs[b * TILE:(b + 1) * TILE, :] = jnp.concatenate([k_ref[s] for s in pair], axis=0)
        v_turned[b] = jnp.transpose(jnp.concatenate([v_ref[s] for s in pair], axis=0))

    def one_query(qb, _):
        srcs = [order_ref[qb * per + u] for u in range(per)]
        q = jnp.concatenate([q_ref[s] for s in srcs], axis=0)
        base = qb * TILE
        starts = start_ref[qb]
        places = base + lax.broadcasted_iota(jnp.int32, (1, TILE), 1)
        group = head_lanes(q.shape)
        for h in range(heads):
            qm[h] = jnp.where(group == h, q, jnp.zeros_like(q))
        down = lax.broadcasted_iota(jnp.int32, (TILE, TILE), 0)

        def scores(kb):
            at = pl.multiple_of(kb * TILE, TILE)
            keys = k_abs[pl.ds(at, TILE), :]
            allowed = jnp.logical_and(down + at >= starts, down + at <= places)
            return [jnp.where(allowed, dot_nt(keys, qm[h]), MASKED) for h in range(heads)]

        found = scores(qb)
        for h in range(heads):
            lanes = slice(h * HEAD_DIM, (h + 1) * HEAD_DIM)
            m = jnp.max(found[h], axis=0, keepdims=True)
            p = jnp.exp(found[h] - m)
            top[h] = m
            tot[h] = jnp.sum(p, axis=0, keepdims=True)
            acc[lanes, :] = dot_nn(v_turned[qb, lanes, :], p.astype(BF))

        def one_key(kb, _):
            found = scores(kb)
            for h in range(heads):
                lanes = slice(h * HEAD_DIM, (h + 1) * HEAD_DIM)
                old = top[h]
                m = jnp.maximum(old, jnp.max(found[h], axis=0, keepdims=True))
                fade = jnp.exp(old - m)
                p = jnp.exp(found[h] - m)
                top[h] = m
                tot[h] = tot[h] * fade + jnp.sum(p, axis=0, keepdims=True)
                acc[lanes, :] = acc[lanes, :] * fade + dot_nn(v_turned[kb, lanes, :], p.astype(BF))
            return 0

        lax.fori_loop(low_ref[qb], qb, one_key, 0)
        for h in range(heads):
            lanes = slice(h * HEAD_DIM, (h + 1) * HEAD_DIM)
            acc[lanes, :] = acc[lanes, :] / tot[h]
            lse_ref[qb, h:h + 1, :] = top[h] + jnp.log(tot[h])
        out = jnp.transpose(acc[...]).astype(BF)
        for u in range(per):
            o_ref[srcs[u]] = out[u * SUB:(u + 1) * SUB]
        return 0

    lax.fori_loop(0, blocks, one_query, 0)


def attend(order, low, q, k, v, start_rows):
    subs, _, cols = q.shape
    length = subs * SUB
    heads = cols // HEAD_DIM
    blocks = length // TILE
    full = [whole(a.shape) for a in (q, k, v, start_rows)]
    return pl.pallas_call(
        attend_kernel,
        grid=(1,),
        in_specs=[SMEM_SPEC, SMEM_SPEC] + full,
        out_specs=[whole(q.shape), whole((blocks, 8, TILE))],
        out_shape=[jax.ShapeDtypeStruct(q.shape, BF), jax.ShapeDtypeStruct((blocks, 8, TILE), F32)],
        scratch_shapes=[VM((length, cols), BF), VM((blocks, cols, TILE), BF), VM((cols, TILE), F32),
                        VM((heads, TILE, cols), BF), VM((heads, 1, TILE), F32), VM((heads, 1, TILE), F32)],
        compiler_params=PARAMS,
        cost_estimate=cost(3 * length * length * cols, 5 * length * cols),
    )(order, low, q, k, v, start_rows)


def attend_back_kernel(order_ref, low_ref, q_ref, k_ref, v_ref, do_ref, o_ref, lse_ref, start_ref,
                       cos_ref, sa_ref, sb_ref, out_ref, sums_ref,
                       k_abs, v_abs, km, dk, dv, dq, qm, dom, stat):
    subs, _, cols = q_ref.shape
    heads = cols // HEAD_DIM
    per = TILE // SUB
    scale = 1.0 / math.sqrt(HEAD_DIM)
    for i in range(subs):
        src = order_ref[i]
        rows = slice(i * SUB, (i + 1) * SUB)
        key = k_ref[src]
        k_abs[rows, :] = key
        v_abs[rows, :] = v_ref[src]
        for h in range(heads):
            km[h, rows, :] = jnp.where(head_lanes(key.shape) == h, key, jnp.zeros_like(key))
        dk[rows, :] = jnp.zeros((SUB, cols), F32)
        dv[rows, :] = jnp.zeros((SUB, cols), F32)
    sums_ref[...] = jnp.zeros(sums_ref.shape, F32)

    def tables(src):
        return cos_ref[src], sa_ref[src], sb_ref[src]

    def emit(src, at, values):
        low = values.astype(BF)
        out_ref[src, :, at:at + cols] = low
        sums_ref[:, at:at + cols] += jnp.sum(low.astype(F32), axis=0, keepdims=True)

    def one_query(qb, _):
        base = pl.multiple_of(qb * TILE, TILE)
        srcs = [order_ref[qb * per + u] for u in range(per)]
        q = jnp.concatenate([q_ref[s] for s in srcs], axis=0)
        do = jnp.concatenate([do_ref[s] for s in srcs], axis=0)
        o = jnp.concatenate([o_ref[s] for s in srcs], axis=0)
        group = head_lanes(q.shape)
        logs = lse_ref[qb]
        inner = jnp.transpose(do.astype(F32) * o.astype(F32))
        for h in range(heads):
            qm[h] = jnp.where(group == h, q, jnp.zeros_like(q))
            dom[h] = jnp.where(group == h, do, jnp.zeros_like(do))
            stat[h, 0:1, :] = logs[h:h + 1, :]
            stat[h, 1:2, :] = jnp.sum(inner[h * HEAD_DIM:(h + 1) * HEAD_DIM, :], axis=0, keepdims=True)
        dq[...] = jnp.zeros((TILE, cols), F32)
        starts = start_ref[qb]
        places = base + lax.broadcasted_iota(jnp.int32, (1, TILE), 1)
        down = lax.broadcasted_iota(jnp.int32, (TILE, TILE), 0)

        def one_key(kb, _):
            at = pl.multiple_of(kb * TILE, TILE)
            keys = k_abs[pl.ds(at, TILE), :]
            vals = v_abs[pl.ds(at, TILE), :]
            allowed = jnp.logical_and(down + at >= starts, down + at <= places)
            dk_new = dv_new = dq_new = None
            more = lambda old, new: new if old is None else old + new
            for h in range(heads):
                s = dot_nt(keys, qm[h])
                p = jnp.exp(jnp.where(allowed, s - stat[h, 0:1, :], MASKED))
                dp = dot_nt(vals, dom[h])
                ds = (p * (dp - stat[h, 1:2, :])).astype(BF)
                dv_new = more(dv_new, dot_nn(p.astype(BF), dom[h]))
                dk_new = more(dk_new, dot_nn(ds, qm[h]))
                dq_new = more(dq_new, dot_tn(ds, km[h, pl.ds(at, TILE), :]))
            dv[pl.ds(at, TILE), :] += dv_new
            dk[pl.ds(at, TILE), :] += dk_new
            dq[...] += dq_new
            return 0

        lax.fori_loop(low_ref[qb], qb + 1, one_key, 0)
        for u in range(per):
            emit(srcs[u], 0, turn(dq[u * SUB:(u + 1) * SUB, :] * scale, tables(srcs[u]), -1.0))
        return 0

    lax.fori_loop(0, subs // per, one_query, 0)
    for i in range(subs):
        src = order_ref[i]
        rows = slice(i * SUB, (i + 1) * SUB)
        emit(src, cols, turn(dk[rows, :], tables(src), -1.0))
        emit(src, 2 * cols, dv[rows, :])


def attend_back(order, low, q, k, v, do, o, lse, start_rows, tables):
    subs, _, cols = q.shape
    length = subs * SUB
    heads = cols // HEAD_DIM
    args = (q, k, v, do, o, lse, start_rows, *tables)
    return pl.pallas_call(
        attend_back_kernel,
        grid=(1,),
        in_specs=[SMEM_SPEC, SMEM_SPEC] + [whole(a.shape) for a in args],
        out_specs=[whole((subs, SUB, 3 * cols)), whole((1, 3 * cols))],
        out_shape=[jax.ShapeDtypeStruct((subs, SUB, 3 * cols), BF), jax.ShapeDtypeStruct((1, 3 * cols), F32)],
        scratch_shapes=[VM((length, cols), BF), VM((length, cols), BF), VM((heads, length, cols), BF),
                        VM((length, cols), F32), VM((length, cols), F32), VM((TILE, cols), F32),
                        VM((heads, TILE, cols), BF), VM((heads, TILE, cols), BF), VM((heads, 2, TILE), F32)],
        compiler_params=PARAMS,
        cost_estimate=cost(8 * length * length * cols, 16 * length * cols),
    )(order, low, *args)


def across(x, k):
    n = lax.axis_size("tensor")
    return lax.ppermute(x, "tensor", [(i, i ^ k) for i in range(n)])


def swap(x):
    return lax.ppermute(x, "pipe", [(0, 1), (1, 0)])


def gather_and_run(x, call, beside=None):
    half = x.shape[0] // 2
    one, two = across(x, 1), across(x, 2)
    kept = call(OWN, [x], None)
    one, two, kept = lax.optimization_barrier((one, two, kept))
    far_a = across(one[:half], 2)
    far_b = across(two[half:], 1)
    kept = call(NEAR, [one, two], kept)
    far_a, far_b, kept, beside = lax.optimization_barrier((far_a, far_b, kept, beside))
    kept = call(FAR, [far_a, far_b], kept)
    return (x, one, two, far_a, far_b), kept, beside


def add_rows(own, got_one, got_two):
    return own + got_one.astype(F32) + got_two.astype(F32)


def dp_reduce(blocks):
    n, rows, cols = blocks.shape
    return lax.psum_scatter(blocks.reshape(n * rows, cols), "dp", scatter_dimension=0, tiled=True)


def butterfly(vec, axis):
    n = lax.axis_size(axis)
    k = 1
    while k < n:
        vec = vec + lax.ppermute(vec, axis, [(i, i ^ k) for i in range(n)])
        k *= 2
    return vec


def flat(a):
    return a.reshape(-1, SUB, a.shape[-1])


NAMES = ("w_qkv", "w_out", "w_in", "w_fc2")


def rows2(a):
    return a.reshape(-1, a.shape[-1])


def forward_layer(x, lp, geo, beside=None):
    call = lambda group, xs, kept: pre_group(group, xs, lp, geo["tables"], kept)
    rows, kept, beside = gather_and_run(x, call, beside)
    n1, n2, q, k, v, g, slope = kept
    o, lse = attend(geo["order"], geo["low"], flat(q), flat(k), flat(v), geo["start_rows"])
    o_slots = o.reshape(q.shape)
    own, far_a, far_b = post_group(ENDS, o_slots, g, lp, [])
    from_one, from_two = across(far_a, 1), across(far_b, 2)
    one, two = post_group(NEAR, o_slots, g, lp, [from_two, from_one])
    summed = add_rows(own, across(one, 1), across(two, 2))
    out_biases = lp["out_bias"].astype(F32)
    result = x.astype(F32) + summed + out_biases[0] + out_biases[1]
    saved = dict(rows=rows, n1=n1, n2=n2, q=flat(q), k=flat(k), v=flat(v), g=g, slope=slope, o=o, lse=lse)
    return result.astype(BF), saved, beside


def over_chip(pair):
    return (pair[0].astype(F32) + swap(pair[1]).astype(F32)).astype(BF)


def backward_layer(e, lp, saved, geo, core, last):
    call = lambda group, es, kept: bpre_group(group, es, saved["slope"], lp, kept)
    _, (e_all, do, df, bin_parts), _ = gather_and_run(e, call)
    early = wgrad_early(core, rows2(saved["o"]), rows2(e_all), rows2(saved["n2"]), rows2(df), rows2(saved["g"]))
    if last:
        early, do = lax.optimization_barrier((over_chip(early), do))
        early = dp_reduce(early)
    dqkv, bqkv_grad = attend_back(geo["order"], geo["low"], saved["q"], saved["k"], saved["v"], flat(do),
                                  saved["o"], saved["lse"], geo["start_rows"], geo["flat_tables"])
    x, x_one, x_two, x_far_a, x_far_b = saved["rows"]
    dqkv_slots = dqkv.reshape(*df.shape[:2], dqkv.shape[-1])
    own, far_a, far_b, sums_a = bpost_group(ENDS, [x, x_far_a, x_far_b], dqkv_slots, df, lp, [])
    from_one, from_two = across(far_a, 1), across(far_b, 2)
    late = wgrad_late(core, rows2(saved["n1"]), rows2(dqkv))
    late, from_one, from_two = lax.optimization_barrier((late, from_one, from_two))
    one, two, sums_b = bpost_group(NEAR, [x_one, x_two], dqkv_slots, df, lp, [from_two, from_one])
    got_one, got_two = across(one, 1), across(two, 2)
    if not last:
        early, got_one, got_two = lax.optimization_barrier((early, got_one, got_two))
        early = dp_reduce(over_chip(early))
    u = add_rows(own, got_one, got_two)
    late = dp_reduce(over_chip(late))
    x_rows, e_rows = x.astype(F32), e.astype(F32)
    normal, inverse_std = norm_rows(x_rows)
    mean_grad = jnp.mean(u, axis=-1, keepdims=True)
    mean_cross = jnp.mean(u * normal, axis=-1, keepdims=True)
    dx = e_rows + (u - mean_grad - normal * mean_cross) * inverse_std
    small = jnp.concatenate([sums_a + sums_b, jnp.sum(e_rows, axis=0, keepdims=True)], axis=0)
    bias_grads = jnp.concatenate([bqkv_grad[0], jnp.sum(bin_parts, axis=(0, 1))])
    return dx.astype(BF), (early, late), small, bias_grads


def unpack_out(g, rows, d):
    groups = d // rows
    return jnp.swapaxes(g.reshape(groups, -1, rows), 0, 1).reshape(-1, d)


def column_order(a, direction):
    shape = a.shape
    heads = shape[-1] // (3 * HEAD_DIM)
    dims = (heads, 3) if direction > 0 else (3, heads)
    split = a.reshape(*shape[:-1], *dims, HEAD_DIM)
    return jnp.swapaxes(split, -2, -3).reshape(shape)


def body(ends, segments, ln_gain, ln_bias, w_qkv, b_qkv, w_out, w_in, b_in, w_fc2, out_bias):
    is_first = lax.axis_index("pipe") == 0
    me = lax.axis_index("tensor")
    n_tensor = lax.axis_size("tensor")
    choose = lambda a, b: jnp.where(is_first, a, b)
    shares = ends[0]
    rows, d = shares.shape[1:]

    got = swap(shares)
    x0 = choose(shares[0], got[1])
    e1 = choose(got[0], shares[1])

    own = dict(ln_gain=ln_gain[0], ln_bias=ln_bias[0], w_qkv=column_order(w_qkv[0], 1),
               b_qkv=column_order(b_qkv, 1), w_out=w_out[0], w_in=w_in[0], b_in=b_in, w_fc2=w_fc2[0],
               out_bias=out_bias[0])
    small_names = ("ln_gain", "ln_bias", "b_qkv", "b_in", "out_bias")
    packed = jnp.concatenate([own[s].reshape(-1) for s in small_names]).reshape(-1, LANES)
    other_packed = swap(packed).reshape(-1)
    other = {name: swap(own[name]) for name in NAMES}
    at = 0
    for s in small_names:
        other[s] = other_packed[at:at + own[s].size].reshape(own[s].shape)
        at += own[s].size
    layer0 = {name: choose(own[name], other[name]) for name in own}
    layer1 = {name: choose(other[name], own[name]) for name in own}

    segment_row = choose(segments[0], segments[1])
    length = segment_row.shape[0]
    places = jnp.arange(length, dtype=jnp.int32)
    begins = jnp.concatenate([jnp.ones((1,), dtype=jnp.bool_), segment_row[1:] != segment_row[:-1]])
    starts = lax.cummax(jnp.where(begins, places, 0), axis=0)
    slot_index = jnp.array(SLOTS, dtype=jnp.int32) ^ me
    by_slot = jnp.take((places - starts).reshape(n_tensor, rows), slot_index, axis=0)
    x0, by_slot = lax.optimization_barrier((x0, by_slot))
    lane = jnp.arange(LANES, dtype=jnp.int32) % HEAD_DIM
    half_rot = ROT // 2
    frequency = jnp.power(10000.0, -2.0 * (lane % half_rot).astype(F32) / ROT)
    angles = by_slot.astype(F32)[:, :, None] * frequency
    sines = jnp.sin(angles)
    tables = (jnp.where(lane < ROT, jnp.cos(angles), 1.0),
              jnp.where(lane < half_rot, -sines, 0.0),
              jnp.where(jnp.logical_and(lane >= half_rot, lane < ROT), sines, 0.0))
    per = rows // SUB
    subs = jnp.arange(length // SUB, dtype=jnp.int32)
    place_of = jnp.array([SLOTS.index(k) for k in range(n_tensor)], dtype=jnp.int32)
    tables = lax.optimization_barrier(tables)
    geo = dict(
        tables=tables,
        flat_tables=[flat(t) for t in tables],
        order=(place_of[(subs // per) ^ me] * per + subs % per).astype(jnp.int32),
        low=(starts.reshape(-1, TILE)[:, 0] // TILE).astype(jnp.int32),
        start_rows=starts.reshape(-1, 1, TILE),
    )

    core = lax.axis_index("pipe").astype(jnp.int32).reshape(1)
    h, saved0, _ = forward_layer(x0, layer0, geo)
    y1, saved1, e1 = forward_layer(h, layer1, geo, e1)
    e0, half1, small1, bias1 = backward_layer(e1, layer1, saved1, geo, core, False)
    dx0, half0, small0, bias0 = backward_layer(e0, layer0, saved0, geo, core, True)

    got = swap(choose(y1, dx0))
    mine = choose(dx0, y1)
    boundary = jnp.stack([choose(mine, got), choose(got, mine)])[None]

    full = []
    for one, zero in zip(half1, half0):
        got = swap(choose(one, zero))
        mine = choose(zero, one)
        full.append((choose(mine, got).astype(F32), choose(got, mine).astype(F32)))
    early, g_qkv = full
    n_out, n_in = w_out.shape[1], w_in.shape[2]
    join = lambda f: jnp.concatenate([f(early[0]), f(early[1])], axis=0)
    g_out = join(lambda a: unpack_out(a[:, :n_out], n_out, d))
    g_in = join(lambda a: a[:, n_out:n_out + n_in])
    g_fc2 = join(lambda a: a[:, n_out + n_in:])
    g_qkv = jnp.concatenate(g_qkv, axis=0)

    n_dp = lax.axis_size("dp")
    small = choose(small0, small1) + swap(choose(small1, small0))
    bias = choose(bias0, bias1) + swap(choose(bias1, bias0))
    at = small.size
    line = butterfly(jnp.concatenate([small.reshape(-1), bias]), "dp")
    small, bias = line[:at].reshape(small.shape), line[at:]
    small = butterfly(small, "tensor").reshape(small.shape[0], n_tensor * n_dp, -1)
    where = lax.axis_index("dp")
    pick = lambda a, i: lax.dynamic_index_in_dim(a, i, -2, keepdims=False)
    sums = pick(small, me * n_dp + where)
    n_qkv = b_qkv.size
    g_b_qkv = pick(column_order(bias[None, :n_qkv], -1).reshape(n_dp, -1), where)
    g_b_in = pick(bias[n_qkv:].reshape(n_dp, -1), where)
    g_gain, g_bias = sums[None, 0:2], sums[None, 2:4]
    g_out_bias = jnp.stack([sums[4], sums[4]])[None]
    return (
        boundary,
        g_gain,
        g_bias,
        column_order(g_qkv, -1)[None],
        g_b_qkv[None],
        g_out[None],
        g_in[None],
        g_b_in[None],
        g_fc2[None],
        g_out_bias,
    )


def solution(mesh):
    placed = (
        P("pipe", "dp", "tensor", None),
        P("dp", None),
        P("pipe", None, None),
        P("pipe", None, None),
        P("pipe", None, "tensor"),
        P("pipe", "tensor"),
        P("pipe", "tensor", None),
        P("pipe", None, "tensor"),
        P("pipe", "tensor"),
        P("pipe", "tensor", None),
        P("pipe", None, None),
    )
    return jax.shard_map(
        body,
        mesh=mesh,
        in_specs=placed,
        out_specs=(
            P("pipe", "dp", "tensor", None),
            P("pipe", None, ("tensor", "dp")),
            P("pipe", None, ("tensor", "dp")),
            P("pipe", "dp", "tensor"),
            P("pipe", ("tensor", "dp")),
            P("pipe", ("tensor", "dp"), None),
            P("pipe", "dp", "tensor"),
            P("pipe", ("tensor", "dp")),
            P("pipe", ("tensor", "dp"), None),
            P("pipe", None, ("tensor", "dp")),
        ),
        check_vma=False,
    )
```

```python
import functools
import math

import jax
import jax.numpy as jnp
from jax import lax
from jax.experimental import pallas as pl
from jax.experimental.pallas import tpu as pltpu
from jax.sharding import PartitionSpec as P

HEAD_DIM = 64
ROT = 16
EPSILON = 1e-05
MASKED = -1e30
TILE = 256
CHUNK = 512
SUB = 128
LANES = 128
BF = jnp.bfloat16
F32 = jnp.float32

VM = pltpu.VMEM
NT = (((1,), (1,)), ((), ()))
TN = (((0,), (0,)), ((), ()))


def dot_nn(a, b):
    return jnp.dot(a, b, preferred_element_type=F32)


def dot_nt(a, b):
    return lax.dot_general(a, b, NT, preferred_element_type=F32)


def dot_tn(a, b):
    return lax.dot_general(a, b, TN, preferred_element_type=F32)


def whole(shape):
    return pl.BlockSpec(shape, lambda *_: (0,) * len(shape))


SMEM_SPEC = pl.BlockSpec(memory_space=pltpu.SMEM)
ANY_SPEC = pl.BlockSpec(memory_space=pl.ANY)
PARAMS = pltpu.CompilerParams(vmem_limit_bytes=56 * 1024 * 1024)


def cost(flops, moved):
    return pl.CostEstimate(flops=int(flops), bytes_accessed=int(moved), transcendentals=0)


def norm_rows(rows):
    centre = jnp.mean(rows, axis=-1, keepdims=True)
    shifted = rows - centre
    inverse_std = lax.rsqrt(jnp.mean(shifted * shifted, axis=-1, keepdims=True) + EPSILON)
    return shifted * inverse_std, inverse_std


def turn(values, tables, direction):
    cos_t, sin_a, sin_b = tables
    width = values.shape[-1]
    times = width // LANES
    wide = lambda t: jnp.concatenate([t] * times, axis=1)
    ahead = pltpu.roll(values, width - ROT // 2, 1)
    behind = pltpu.roll(values, ROT // 2, 1)
    return values * wide(cos_t) + direction * (ahead * wide(sin_a) + behind * wide(sin_b))


SLOTS = (1, 2, 0, 3)
OWN, NEAR, FAR, ENDS = (1, 2), (2, 0), (1, 3), (2, 1)


def stacked(refs):
    parts = [r[...] for r in refs]
    return parts[0] if len(parts) == 1 else jnp.concatenate(parts, axis=0)


def pre_kernel(n_x, n_alias, *refs):
    x_refs = refs[:n_x]
    (gain_ref, bias_ref, wqkv_ref, bqkv_ref, win_ref, bin_ref, cos_ref, sa_ref, sb_ref) = refs[n_x:n_x + 9]
    n1_ref, n2_ref, q_ref, k_ref, v_ref, g_ref, slope_ref, n2_keep = refs[n_x + 9 + n_alias:]

    @pl.when(pl.program_id(0) == 0)
    def _():
        normal, _ = norm_rows(stacked(x_refs).astype(F32))
        gains = gain_ref[...].astype(F32)
        biases = bias_ref[...].astype(F32)
        n1 = (normal * gains[0:1] + biases[0:1]).astype(BF)
        n2 = (normal * gains[1:2] + biases[1:2]).astype(BF)
        n1_ref[...] = n1.reshape(n1_ref.shape)
        n2_ref[...] = n2.reshape(n2_ref.shape)
        n2_keep[...] = n2
        flat = lambda r: r[...].reshape(n1.shape[0], LANES)
        tables = (flat(cos_ref), flat(sa_ref), flat(sb_ref))
        wide = q_ref.shape[-1]
        scale = 1.0 / math.sqrt(HEAD_DIM)
        bq = bqkv_ref[...].astype(F32)
        part = lambda i: dot_nn(n1, wqkv_ref[:, i * wide:(i + 1) * wide]) + bq[:, i * wide:(i + 1) * wide]
        q = (turn(part(0), tables, 1.0).astype(BF).astype(F32) * scale).astype(BF)
        q_ref[...] = q.reshape(q_ref.shape)
        k_ref[...] = turn(part(1), tables, 1.0).astype(BF).reshape(k_ref.shape)
        v_ref[...] = part(2).astype(BF).reshape(v_ref.shape)

    f = dot_nn(n2_keep[...], win_ref[...]) + bin_ref[...].astype(F32)
    phi = 0.5 * (1.0 + lax.erf(f * (1.0 / math.sqrt(2.0))))
    density = jnp.exp(-0.5 * f * f) * (1.0 / math.sqrt(2.0 * math.pi))
    g_ref[...] = (f * phi).astype(BF).reshape(g_ref.shape)
    slope_ref[...] = (phi + f * density).astype(BF).reshape(slope_ref.shape)


def group_call(kernel, args, in_specs, outs, kept, grid, scratch, price):
    n_alias = 0 if kept is None else len(outs)
    specs = list(in_specs)
    operands = list(args)
    aliases = {}
    if kept is not None:
        for i, buf in enumerate(kept):
            aliases[len(operands)] = i
            operands.append(buf)
            specs.append(ANY_SPEC)
    return pl.pallas_call(
        functools.partial(kernel, n_alias),
        grid=grid,
        in_specs=specs,
        out_specs=[pl.BlockSpec(block, index) for _, _, block, index in outs],
        out_shape=[jax.ShapeDtypeStruct(shape, dtype) for shape, dtype, _, _ in outs],
        input_output_aliases=aliases,
        scratch_shapes=scratch,
        compiler_params=PARAMS,
        cost_estimate=price,
    )(*operands)


def pre_group(group, xs, lp, tables, kept):
    size, at = group
    d = xs[0].shape[1]
    slots, rows = len(SLOTS), tables[0].shape[1]
    total = size * rows
    wide = lp["w_qkv"].shape[1]
    units = lp["w_in"].shape[1]
    cols = wide // 3
    ck = min(CHUNK, units)
    first = lambda j: (at, 0, 0)
    moving = lambda j: (at, 0, j)
    outs = [((slots, rows, d), BF, (size, rows, d), first)] * 2
    outs += [((slots, rows, cols), BF, (size, rows, cols), first)] * 3
    outs += [((slots, rows, units), BF, (size, rows, ck), moving)] * 2
    in_specs = [whole(x.shape) for x in xs]
    in_specs += [whole((2, d)), whole((2, d)), whole((d, wide)), whole((1, wide)),
                 pl.BlockSpec((d, ck), lambda j: (0, j)), pl.BlockSpec((1, ck), lambda j: (0, j))]
    in_specs += [pl.BlockSpec((size, rows, LANES), first)] * 3
    args = [*xs, lp["ln_gain"], lp["ln_bias"], lp["w_qkv"], lp["b_qkv"], lp["w_in"], lp["b_in"], *tables]
    return group_call(functools.partial(pre_kernel, len(xs)), args, in_specs, outs, kept, (units // ck,),
                      [VM((total, d), BF)],
                      cost(2 * total * d * (wide + units), 2 * d * (wide + units) + 10 * total * d))


def share(part, addend_refs, outs):
    if len(outs) == 3:
        own, far_a, far_b = outs
        rows, half = own.shape[0], far_a.shape[0]
        own[...] = part[:rows]
        far_a[...] = part[rows:rows + half].astype(BF)
        far_b[...] = part[rows + half:].astype(BF)
        return
    one, two = outs
    from_two, from_one = addend_refs
    rows, half = one.shape[0], from_two.shape[0]
    one[:half, :] = part[:half].astype(BF)
    one[half:, :] = (part[half:rows] + from_two[...].astype(F32)).astype(BF)
    two[:half, :] = (part[rows:rows + half] + from_one[...].astype(F32)).astype(BF)
    two[half:, :] = part[rows + half:].astype(BF)


def share_specs(group, rows, d, ck):
    col = lambda j: (0, j)
    if group == ENDS:
        shapes = [((rows, d), F32), ((rows // 2, d), BF), ((rows // 2, d), BF)]
    else:
        shapes = [((rows, d), BF), ((rows, d), BF)]
    return [pl.BlockSpec((s[0], ck), col) for s, _ in shapes], [jax.ShapeDtypeStruct(s, t) for s, t in shapes]


def post_kernel(n_add, o_ref, g_ref, wout_ref, wfc_ref, *rest):
    total = o_ref.shape[0] * o_ref.shape[1]
    o = o_ref[...].reshape(total, o_ref.shape[-1])
    g = g_ref[...].reshape(total, g_ref.shape[-1])
    share(dot_nn(o, wout_ref[...]) + dot_nn(g, wfc_ref[...]), rest[:n_add], rest[n_add:])


def post_group(group, o_all, g_all, lp, addends):
    size, at = group
    _, rows, cols = o_all.shape
    units, d = lp["w_fc2"].shape
    ck = min(CHUNK, d)
    fixed = lambda j: (at, 0, 0)
    in_specs = [pl.BlockSpec((size, rows, cols), fixed), pl.BlockSpec((size, rows, units), fixed),
                pl.BlockSpec((cols, ck), lambda j: (0, j)), pl.BlockSpec((units, ck), lambda j: (0, j))]
    in_specs += [pl.BlockSpec((a.shape[0], ck), lambda j: (0, j)) for a in addends]
    out_specs, out_shape = share_specs(group, rows, d, ck)
    total = size * rows
    return pl.pallas_call(
        functools.partial(post_kernel, len(addends)),
        grid=(d // ck,),
        in_specs=in_specs,
        out_specs=out_specs,
        out_shape=out_shape,
        compiler_params=PARAMS,
        cost_estimate=cost(2 * total * d * (cols + units), 2 * d * (cols + units) + 5 * total * d),
    )(o_all, g_all, lp["w_out"], lp["w_fc2"], *addends)


def bpre_kernel(n_x, n_alias, *refs):
    e_refs = refs[:n_x]
    wout_ref, wfc_ref, slope_ref = refs[n_x:n_x + 3]
    eall_ref, do_ref, df_ref, sums_ref = refs[n_x + 3 + n_alias:]
    e = stacked(e_refs)

    @pl.when(pl.program_id(0) == 0)
    def _():
        eall_ref[...] = e.reshape(eall_ref.shape)
        do_ref[...] = dot_nt(e, wout_ref[...]).astype(BF).reshape(do_ref.shape)

    back = dot_nt(e, wfc_ref[...])
    df = (back * slope_ref[...].reshape(back.shape).astype(F32)).astype(BF)
    df_ref[...] = df.reshape(df_ref.shape)
    sums = jnp.sum(df.astype(F32).reshape(df_ref.shape), axis=1, keepdims=True)
    sums_ref[...] = sums


def bpre_group(group, es, slope_all, lp, kept):
    size, at = group
    d = es[0].shape[1]
    slots, rows, units = slope_all.shape
    cols = lp["w_out"].shape[0]
    ck = min(CHUNK, units)
    first = lambda j: (at, 0, 0)
    moving = lambda j: (at, 0, j)
    outs = [((slots, rows, d), BF, (size, rows, d), first), ((slots, rows, cols), BF, (size, rows, cols), first),
            ((slots, rows, units), BF, (size, rows, ck), moving), ((slots, 1, units), F32, (size, 1, ck), moving)]
    in_specs = [whole(e.shape) for e in es]
    in_specs += [whole((cols, d)), pl.BlockSpec((ck, d), lambda j: (j, 0)),
                 pl.BlockSpec((size, rows, ck), moving)]
    args = [*es, lp["w_out"], lp["w_fc2"], slope_all]
    total = size * rows
    return group_call(functools.partial(bpre_kernel, len(es)), args, in_specs, outs, kept, (units // ck,), [],
                      cost(2 * total * d * (cols + units), 2 * d * (cols + units) + 8 * total * d))


def bpost_kernel(n_x, n_add, ck, *refs):
    x_refs = refs[:n_x]
    gain_ref, dqkv_ref, df_ref, wqkv_ref, win_ref = refs[n_x:n_x + 5]
    addend_refs = refs[n_x + 5:n_x + 5 + n_add]
    outs = refs[n_x + 5 + n_add:-2]
    sums_ref, normal_keep = refs[-2:]
    j = pl.program_id(0)

    @pl.when(j == 0)
    def _():
        normal, _ = norm_rows(stacked(x_refs).astype(F32))
        for c in range(normal_keep.shape[0]):
            normal_keep[c] = normal[:, c * ck:(c + 1) * ck]

    normal = normal_keep[j]
    flat = lambda r: r[...].reshape(normal.shape[0], r.shape[-1])
    one = dot_nt(flat(dqkv_ref), wqkv_ref[...])
    two = dot_nt(flat(df_ref), win_ref[...])
    total = lambda v: jnp.sum(v, axis=0, keepdims=True)
    sums_ref[0:1, :] = total(one * normal)
    sums_ref[1:2, :] = total(two * normal)
    sums_ref[2:3, :] = total(one)
    sums_ref[3:4, :] = total(two)
    gains = gain_ref[...].astype(F32)
    share(one * gains[0:1] + two * gains[1:2], addend_refs, outs)


def bpost_group(group, xs, dqkv_all, df_all, lp, addends):
    size, at = group
    d = xs[0].shape[1]
    _, rows, wide = dqkv_all.shape
    units = df_all.shape[-1]
    ck = min(CHUNK, d)
    total = size * rows
    fixed = lambda j: (at, 0, 0)
    in_specs = [whole(x.shape) for x in xs]
    in_specs += [pl.BlockSpec((2, ck), lambda j: (0, j)),
                 pl.BlockSpec((size, rows, wide), fixed), pl.BlockSpec((size, rows, units), fixed),
                 pl.BlockSpec((ck, wide), lambda j: (j, 0)), pl.BlockSpec((ck, units), lambda j: (j, 0))]
    in_specs += [pl.BlockSpec((a.shape[0], ck), lambda j: (0, j)) for a in addends]
    out_specs, out_shape = share_specs(group, rows, d, ck)
    return pl.pallas_call(
        functools.partial(bpost_kernel, len(xs), len(addends), ck),
        grid=(d // ck,),
        in_specs=in_specs,
        out_specs=out_specs + [pl.BlockSpec((4, ck), lambda j: (0, j))],
        out_shape=out_shape + [jax.ShapeDtypeStruct((4, d), F32)],
        scratch_shapes=[VM((d // ck, total, ck), F32)],
        compiler_params=PARAMS,
        cost_estimate=cost(2 * total * d * (wide + units), 2 * d * (wide + units) + 7 * total * d),
    )(*xs, lp["ln_gain"], dqkv_all, df_all, lp["w_qkv"], lp["w_in"], *addends)


def wgrad_kernel(with_out, core_ref, *refs):
    first = core_ref[0] == 0
    if with_out:
        keep_ref, give_ref, whole_out = refs[-3:]
        pairs = list(refs[2:-3])
    else:
        keep_ref, give_ref = refs[-2:]
        pairs = list(refs[:-2])
    many, half, _ = keep_ref.shape

    def store(b, rows, cols, zero, one):
        keep_ref[b, rows, cols] = jnp.where(first, zero, one).astype(BF)
        give_ref[b, rows, cols] = jnp.where(first, one, zero).astype(BF)

    at = 0
    if with_out:
        o_ref, e_ref = refs[:2]
        cols = o_ref.shape[1]
        j = pl.program_id(0)

        @pl.when(j == 0)
        def _():
            whole_out[...] = dot_tn(o_ref[...], e_ref[...])

        groups = e_ref.shape[1] // cols
        few = half // groups
        for b in range(many):
            start = 2 * (j * many + b)
            zero, one = [whole_out[pl.ds(pl.multiple_of((start + h) * few, few), few), :] for h in range(2)]
            for c in range(groups):
                part = slice(c * cols, (c + 1) * cols)
                store(b, slice(c * few, (c + 1) * few), slice(0, cols), zero[:, part], one[:, part])
        at = cols
        pairs.append(e_ref)
    for a_ref, b_ref in zip(pairs[0::2], pairs[1::2]):
        wide = b_ref.shape[1]
        product = dot_tn(a_ref[...], b_ref[...])
        for b in range(many):
            low = 2 * b * half
            store(b, slice(None), slice(at, at + wide), product[low:low + half], product[low + half:low + 2 * half])
        at += wide


def wgrad_shapes(d, cols):
    n = lax.axis_size("dp")
    block = d // n
    lanes = max(block, LANES)
    many = lanes // block
    specs = [pl.BlockSpec((many, block // 2, cols), lambda j: (j, 0, 0))] * 2
    shapes = [jax.ShapeDtypeStruct((n, block // 2, cols), BF)] * 2
    return d // lanes, lanes, specs, shapes


def wgrad_early(core, o, e, n2, df, g):
    length, d = e.shape
    cols = o.shape[1] + df.shape[1] + d
    steps, lanes, specs, shapes = wgrad_shapes(d, cols)
    moving = pl.BlockSpec((length, lanes), lambda j: (0, j))
    return pl.pallas_call(
        functools.partial(wgrad_kernel, True),
        grid=(steps,),
        in_specs=[SMEM_SPEC, whole(o.shape), whole(e.shape), moving, whole(df.shape), moving],
        out_specs=specs,
        out_shape=shapes,
        scratch_shapes=[VM((o.shape[1], d), F32)],
        compiler_params=PARAMS,
        cost_estimate=cost(2 * length * d * cols, 2 * length * 4 * d + 2 * d * cols),
    )(core, o, e, n2, df, g)


def wgrad_late(core, n1, dqkv):
    length, d = n1.shape
    cols = dqkv.shape[1]
    steps, lanes, specs, shapes = wgrad_shapes(d, cols)
    return pl.pallas_call(
        functools.partial(wgrad_kernel, False),
        grid=(steps,),
        in_specs=[SMEM_SPEC, pl.BlockSpec((length, lanes), lambda j: (0, j)), whole(dqkv.shape)],
        out_specs=specs,
        out_shape=shapes,
        compiler_params=PARAMS,
        cost_estimate=cost(2 * length * d * cols, 2 * length * 2 * d + 2 * d * cols),
    )(core, n1, dqkv)


def head_lanes(shape):
    return lax.broadcasted_iota(jnp.int32, shape, len(shape) - 1) // HEAD_DIM


def attend_kernel(order_ref, low_ref, q_ref, k_ref, v_ref, start_ref, o_ref, lse_ref,
                  k_abs, v_turned, acc, qm, top, tot):
    subs, _, cols = q_ref.shape
    heads = cols // HEAD_DIM
    per = TILE // SUB
    blocks = subs // per
    for b in range(blocks):
        pair = [order_ref[b * per + u] for u in range(per)]
        k_abs[b * TILE:(b + 1) * TILE, :] = jnp.concatenate([k_ref[s] for s in pair], axis=0)
        v_turned[b] = jnp.transpose(jnp.concatenate([v_ref[s] for s in pair], axis=0))

    def one_query(qb, _):
        srcs = [order_ref[qb * per + u] for u in range(per)]
        q = jnp.concatenate([q_ref[s] for s in srcs], axis=0)
        base = qb * TILE
        starts = start_ref[qb]
        places = base + lax.broadcasted_iota(jnp.int32, (1, TILE), 1)
        group = head_lanes(q.shape)
        for h in range(heads):
            qm[h] = jnp.where(group == h, q, jnp.zeros_like(q))
        down = lax.broadcasted_iota(jnp.int32, (TILE, TILE), 0)

        def scores(kb):
            at = pl.multiple_of(kb * TILE, TILE)
            keys = k_abs[pl.ds(at, TILE), :]
            allowed = jnp.logical_and(down + at >= starts, down + at <= places)
            return [jnp.where(allowed, dot_nt(keys, qm[h]), MASKED) for h in range(heads)]

        found = scores(qb)
        for h in range(heads):
            lanes = slice(h * HEAD_DIM, (h + 1) * HEAD_DIM)
            m = jnp.max(found[h], axis=0, keepdims=True)
            p = jnp.exp(found[h] - m)
            top[h] = m
            tot[h] = jnp.sum(p, axis=0, keepdims=True)
            acc[lanes, :] = dot_nn(v_turned[qb, lanes, :], p.astype(BF))

        def one_key(kb, _):
            found = scores(kb)
            for h in range(heads):
                lanes = slice(h * HEAD_DIM, (h + 1) * HEAD_DIM)
                old = top[h]
                m = jnp.maximum(old, jnp.max(found[h], axis=0, keepdims=True))
                fade = jnp.exp(old - m)
                p = jnp.exp(found[h] - m)
                top[h] = m
                tot[h] = tot[h] * fade + jnp.sum(p, axis=0, keepdims=True)
                acc[lanes, :] = acc[lanes, :] * fade + dot_nn(v_turned[kb, lanes, :], p.astype(BF))
            return 0

        lax.fori_loop(low_ref[qb], qb, one_key, 0)
        for h in range(heads):
            lanes = slice(h * HEAD_DIM, (h + 1) * HEAD_DIM)
            acc[lanes, :] = acc[lanes, :] / tot[h]
            lse_ref[qb, h:h + 1, :] = top[h] + jnp.log(tot[h])
        out = jnp.transpose(acc[...]).astype(BF)
        for u in range(per):
            o_ref[srcs[u]] = out[u * SUB:(u + 1) * SUB]
        return 0

    lax.fori_loop(0, blocks, one_query, 0)


def attend(order, low, q, k, v, start_rows):
    subs, _, cols = q.shape
    length = subs * SUB
    heads = cols // HEAD_DIM
    blocks = length // TILE
    full = [whole(a.shape) for a in (q, k, v, start_rows)]
    return pl.pallas_call(
        attend_kernel,
        grid=(1,),
        in_specs=[SMEM_SPEC, SMEM_SPEC] + full,
        out_specs=[whole(q.shape), whole((blocks, 8, TILE))],
        out_shape=[jax.ShapeDtypeStruct(q.shape, BF), jax.ShapeDtypeStruct((blocks, 8, TILE), F32)],
        scratch_shapes=[VM((length, cols), BF), VM((blocks, cols, TILE), BF), VM((cols, TILE), F32),
                        VM((heads, TILE, cols), BF), VM((heads, 1, TILE), F32), VM((heads, 1, TILE), F32)],
        compiler_params=PARAMS,
        cost_estimate=cost(3 * length * length * cols, 5 * length * cols),
    )(order, low, q, k, v, start_rows)


def attend_back_kernel(order_ref, low_ref, q_ref, k_ref, v_ref, do_ref, o_ref, lse_ref, start_ref,
                       cos_ref, sa_ref, sb_ref, out_ref, sums_ref,
                       k_abs, v_abs, km, dk, dv, dq, qm, dom, stat):
    subs, _, cols = q_ref.shape
    heads = cols // HEAD_DIM
    per = TILE // SUB
    scale = 1.0 / math.sqrt(HEAD_DIM)
    for i in range(subs):
        src = order_ref[i]
        rows = slice(i * SUB, (i + 1) * SUB)
        key = k_ref[src]
        k_abs[rows, :] = key
        v_abs[rows, :] = v_ref[src]
        for h in range(heads):
            km[h, rows, :] = jnp.where(head_lanes(key.shape) == h, key, jnp.zeros_like(key))
        dk[rows, :] = jnp.zeros((SUB, cols), F32)
        dv[rows, :] = jnp.zeros((SUB, cols), F32)
    sums_ref[...] = jnp.zeros(sums_ref.shape, F32)

    def tables(src):
        return cos_ref[src], sa_ref[src], sb_ref[src]

    def emit(src, at, values):
        low = values.astype(BF)
        out_ref[src, :, at:at + cols] = low
        sums_ref[:, at:at + cols] += jnp.sum(low.astype(F32), axis=0, keepdims=True)

    def one_query(qb, _):
        base = pl.multiple_of(qb * TILE, TILE)
        srcs = [order_ref[qb * per + u] for u in range(per)]
        q = jnp.concatenate([q_ref[s] for s in srcs], axis=0)
        do = jnp.concatenate([do_ref[s] for s in srcs], axis=0)
        o = jnp.concatenate([o_ref[s] for s in srcs], axis=0)
        group = head_lanes(q.shape)
        logs = lse_ref[qb]
        inner = jnp.transpose(do.astype(F32) * o.astype(F32))
        for h in range(heads):
            qm[h] = jnp.where(group == h, q, jnp.zeros_like(q))
            dom[h] = jnp.where(group == h, do, jnp.zeros_like(do))
            stat[h, 0:1, :] = logs[h:h + 1, :]
            stat[h, 1:2, :] = jnp.sum(inner[h * HEAD_DIM:(h + 1) * HEAD_DIM, :], axis=0, keepdims=True)
        dq[...] = jnp.zeros((TILE, cols), F32)
        starts = start_ref[qb]
        places = base + lax.broadcasted_iota(jnp.int32, (1, TILE), 1)
        down = lax.broadcasted_iota(jnp.int32, (TILE, TILE), 0)

        def one_key(kb, _):
            at = pl.multiple_of(kb * TILE, TILE)
            keys = k_abs[pl.ds(at, TILE), :]
            vals = v_abs[pl.ds(at, TILE), :]
            allowed = jnp.logical_and(down + at >= starts, down + at <= places)
            dk_new = dv_new = dq_new = None
            more = lambda old, new: new if old is None else old + new
            for h in range(heads):
                s = dot_nt(keys, qm[h])
                p = jnp.exp(jnp.where(allowed, s - stat[h, 0:1, :], MASKED))
                dp = dot_nt(vals, dom[h])
                ds = (p * (dp - stat[h, 1:2, :])).astype(BF)
                dv_new = more(dv_new, dot_nn(p.astype(BF), dom[h]))
                dk_new = more(dk_new, dot_nn(ds, qm[h]))
                dq_new = more(dq_new, dot_tn(ds, km[h, pl.ds(at, TILE), :]))
            dv[pl.ds(at, TILE), :] += dv_new
            dk[pl.ds(at, TILE), :] += dk_new
            dq[...] += dq_new
            return 0

        lax.fori_loop(low_ref[qb], qb + 1, one_key, 0)
        for u in range(per):
            emit(srcs[u], 0, turn(dq[u * SUB:(u + 1) * SUB, :] * scale, tables(srcs[u]), -1.0))
        return 0

    lax.fori_loop(0, subs // per, one_query, 0)
    for i in range(subs):
        src = order_ref[i]
        rows = slice(i * SUB, (i + 1) * SUB)
        emit(src, cols, turn(dk[rows, :], tables(src), -1.0))
        emit(src, 2 * cols, dv[rows, :])


def attend_back(order, low, q, k, v, do, o, lse, start_rows, tables):
    subs, _, cols = q.shape
    length = subs * SUB
    heads = cols // HEAD_DIM
    args = (q, k, v, do, o, lse, start_rows, *tables)
    return pl.pallas_call(
        attend_back_kernel,
        grid=(1,),
        in_specs=[SMEM_SPEC, SMEM_SPEC] + [whole(a.shape) for a in args],
        out_specs=[whole((subs, SUB, 3 * cols)), whole((1, 3 * cols))],
        out_shape=[jax.ShapeDtypeStruct((subs, SUB, 3 * cols), BF), jax.ShapeDtypeStruct((1, 3 * cols), F32)],
        scratch_shapes=[VM((length, cols), BF), VM((length, cols), BF), VM((heads, length, cols), BF),
                        VM((length, cols), F32), VM((length, cols), F32), VM((TILE, cols), F32),
                        VM((heads, TILE, cols), BF), VM((heads, TILE, cols), BF), VM((heads, 2, TILE), F32)],
        compiler_params=PARAMS,
        cost_estimate=cost(8 * length * length * cols, 16 * length * cols),
    )(order, low, *args)


def across(x, k):
    n = lax.axis_size("tensor")
    return lax.ppermute(x, "tensor", [(i, i ^ k) for i in range(n)])


def swap(x):
    return lax.ppermute(x, "pipe", [(0, 1), (1, 0)])


def gather_and_run(x, call, beside=None, near=None):
    half = x.shape[0] // 2
    one, two = across(x, 1), across(x, 2)
    kept = call(OWN, [x], None)
    one, two, kept = lax.optimization_barrier((one, two, kept))
    far_a = across(one[:half], 2)
    far_b = across(two[half:], 1)
    kept = call(NEAR, [one, two], kept)
    if near is not None:
        kept = near(kept)
    far_a, far_b, kept, beside = lax.optimization_barrier((far_a, far_b, kept, beside))
    kept = call(FAR, [far_a, far_b], kept)
    return (x, one, two, far_a, far_b), kept, beside


def add_rows(own, got_one, got_two):
    return own + got_one.astype(F32) + got_two.astype(F32)


def dp_reduce(blocks):
    n, rows, cols = blocks.shape
    return lax.psum_scatter(blocks.reshape(n * rows, cols), "dp", scatter_dimension=0, tiled=True)


def butterfly(vec, axis):
    n = lax.axis_size(axis)
    k = 1
    while k < n:
        vec = vec + lax.ppermute(vec, axis, [(i, i ^ k) for i in range(n)])
        k *= 2
    return vec


def flat(a):
    return a.reshape(-1, SUB, a.shape[-1])


NAMES = ("w_qkv", "w_out", "w_in", "w_fc2")


def rows2(a):
    return a.reshape(-1, a.shape[-1])


def tie(*values):
    return lax.optimization_barrier(values)


def forward_layer(x, lp, geo, beside=None):
    call = lambda group, xs, kept: pre_group(group, xs, lp, geo["tables"], kept)
    rows, kept, beside = gather_and_run(x, call, beside)
    n1, n2, q, k, v, g, slope = kept
    o, lse = attend(geo["order"], geo["low"], flat(q), flat(k), flat(v), geo["start_rows"])
    saved = dict(rows=rows, n1=n1, n2=n2, q=flat(q), k=flat(k), v=flat(v), g=g, slope=slope, o=o, lse=lse)
    return saved, beside


def branches(saved, lp):
    g = saved["g"]
    o_slots = saved["o"].reshape(*g.shape[:2], -1)
    own, far_a, far_b = post_group(ENDS, o_slots, g, lp, [])
    from_one, from_two = across(far_a, 1), across(far_b, 2)
    one, two = post_group(NEAR, o_slots, g, lp, [from_two, from_one])
    return own, one, two


def layer_result(saved, lp, own, got_one, got_two):
    out_biases = lp["out_bias"].astype(F32)
    summed = add_rows(own, got_one, got_two)
    return (saved["rows"][0].astype(F32) + summed + out_biases[0] + out_biases[1]).astype(BF)


def over_chip(pair):
    return (pair[0].astype(F32) + swap(pair[1]).astype(F32)).astype(BF)


def input_grad(e, x, u):
    x_rows, e_rows = x.astype(F32), e.astype(F32)
    normal, inverse_std = norm_rows(x_rows)
    mean_grad = jnp.mean(u, axis=-1, keepdims=True)
    mean_cross = jnp.mean(u * normal, axis=-1, keepdims=True)
    return (e_rows + (u - mean_grad - normal * mean_cross) * inverse_std).astype(BF)


def back_attention(saved, do, geo):
    return attend_back(geo["order"], geo["low"], saved["q"], saved["k"], saved["v"], flat(do),
                       saved["o"], saved["lse"], geo["start_rows"], geo["flat_tables"])


def backward_layer(e, lp, saved, geo, core, before=None, after=None, near=None, ending=None):
    last = ending is not None
    call = lambda group, es, kept: bpre_group(group, es, saved["slope"], lp, kept)
    _, kept, _ = gather_and_run(e, call, near=near)
    e_all, do, df, bin_parts = kept
    early = wgrad_early(core, rows2(saved["o"]), rows2(e_all), rows2(saved["n2"]), rows2(df), rows2(saved["g"]))
    if before is not None:
        do = before(do)
    if last:
        early, do = tie(over_chip(early), do)
        early = dp_reduce(early)
    dqkv, bqkv_grad = back_attention(saved, do, geo)
    if after is not None:
        dqkv = after(dqkv)
    x, x_one, x_two, x_far_a, x_far_b = saved["rows"]
    dqkv_slots = dqkv.reshape(*df.shape[:2], dqkv.shape[-1])
    own, far_a, far_b, sums_a = bpost_group(ENDS, [x, x_far_a, x_far_b], dqkv_slots, df, lp, [])
    from_one, from_two = across(far_a, 1), across(far_b, 2)
    late = wgrad_late(core, rows2(saved["n1"]), rows2(dqkv))
    late, from_one, from_two = tie(late, from_one, from_two)
    one, two, sums_b = bpost_group(NEAR, [x_one, x_two], dqkv_slots, df, lp, [from_two, from_one])
    got_one, got_two = across(one, 1), across(two, 2)
    late = over_chip(late)
    small = jnp.concatenate([sums_a + sums_b, jnp.sum(e.astype(F32), axis=0, keepdims=True)], axis=0)
    bias_grads = jnp.concatenate([bqkv_grad[0], jnp.sum(bin_parts, axis=(0, 1))])
    small = (small, bias_grads)
    if last:
        early, late = tie(early, late)
        small = ending(small)
        small, got_one, got_two = tie(small, got_one, got_two)
    else:
        early, got_one, got_two = tie(early, got_one, got_two)
        early = dp_reduce(over_chip(early))
    late = dp_reduce(late)
    dx = input_grad(e, x, add_rows(own, got_one, got_two))
    return dx, early, late, small


def unpack_out(g, rows, d):
    groups = d // rows
    return jnp.swapaxes(g.reshape(groups, -1, rows), 0, 1).reshape(-1, d)


def column_order(a, direction):
    shape = a.shape
    heads = shape[-1] // (3 * HEAD_DIM)
    dims = (heads, 3) if direction > 0 else (3, heads)
    split = a.reshape(*shape[:-1], *dims, HEAD_DIM)
    return jnp.swapaxes(split, -2, -3).reshape(shape)


def body(ends, segments, ln_gain, ln_bias, w_qkv, b_qkv, w_out, w_in, b_in, w_fc2, out_bias):
    is_first = lax.axis_index("pipe") == 0
    me = lax.axis_index("tensor")
    n_tensor = lax.axis_size("tensor")
    choose = lambda a, b: jnp.where(is_first, a, b)
    shares = ends[0]
    rows, d = shares.shape[1:]

    got = swap(shares)
    x0 = choose(shares[0], got[1])
    e1 = choose(got[0], shares[1])

    own = dict(ln_gain=ln_gain[0], ln_bias=ln_bias[0], w_qkv=column_order(w_qkv[0], 1),
               b_qkv=column_order(b_qkv, 1), w_out=w_out[0], w_in=w_in[0], b_in=b_in, w_fc2=w_fc2[0],
               out_bias=out_bias[0])
    own, x0, e1 = tie(own, x0, e1)
    small_names = ("ln_gain", "ln_bias", "b_qkv", "b_in", "out_bias")
    packed = jnp.concatenate([own[s].reshape(-1) for s in small_names]).reshape(-1, LANES)
    other_packed = swap(packed).reshape(-1)
    other = {name: swap(own[name]) for name in NAMES}
    at = 0
    for s in small_names:
        other[s] = other_packed[at:at + own[s].size].reshape(own[s].shape)
        at += own[s].size
    layer0 = {name: choose(own[name], other[name]) for name in own}
    layer1 = {name: choose(other[name], own[name]) for name in own}

    segment_row = choose(segments[0], segments[1])
    length = segment_row.shape[0]
    places = jnp.arange(length, dtype=jnp.int32)
    begins = jnp.concatenate([jnp.ones((1,), dtype=jnp.bool_), segment_row[1:] != segment_row[:-1]])
    starts = lax.cummax(jnp.where(begins, places, 0), axis=0)
    slot_index = jnp.array(SLOTS, dtype=jnp.int32) ^ me
    by_slot = jnp.take((places - starts).reshape(n_tensor, rows), slot_index, axis=0)
    x0, by_slot = lax.optimization_barrier((x0, by_slot))
    lane = jnp.arange(LANES, dtype=jnp.int32) % HEAD_DIM
    half_rot = ROT // 2
    frequency = jnp.power(10000.0, -2.0 * (lane % half_rot).astype(F32) / ROT)
    angles = by_slot.astype(F32)[:, :, None] * frequency
    sines = jnp.sin(angles)
    tables = (jnp.where(lane < ROT, jnp.cos(angles), 1.0),
              jnp.where(lane < half_rot, -sines, 0.0),
              jnp.where(jnp.logical_and(lane >= half_rot, lane < ROT), sines, 0.0))
    per = rows // SUB
    subs = jnp.arange(length // SUB, dtype=jnp.int32)
    place_of = jnp.array([SLOTS.index(k) for k in range(n_tensor)], dtype=jnp.int32)
    tables = lax.optimization_barrier(tables)
    geo = dict(
        tables=tables,
        flat_tables=[flat(t) for t in tables],
        order=(place_of[(subs // per) ^ me] * per + subs % per).astype(jnp.int32),
        low=(starts.reshape(-1, TILE)[:, 0] // TILE).astype(jnp.int32),
        start_rows=starts.reshape(-1, 1, TILE),
    )

    core = lax.axis_index("pipe").astype(jnp.int32).reshape(1)
    saved0, _ = forward_layer(x0, layer0, geo)
    own, one, two = branches(saved0, layer0)
    h = layer_result(saved0, layer0, own, across(one, 1), across(two, 2))
    saved1, e1 = forward_layer(h, layer1, geo, e1)

    to_next = lambda a: lax.ppermute(a, "pipe", [(0, 1)])
    to_first = lambda a: lax.ppermute(a, "pipe", [(1, 0)])
    held = {}

    def send_result(do):
        own, one, two = branches(saved1, layer1)
        one, two, do = tie(one, two, do)
        held["y"] = own, across(one, 1), across(two, 2)
        return do

    def take_result(dqkv):
        own, got_one, got_two = held["y"]
        got_one, got_two, dqkv = tie(got_one, got_two, dqkv)
        y1 = layer_result(saved1, layer1, own, got_one, got_two)
        held["y1"] = y1, to_next(y1)
        return dqkv

    e0, early1, late1, small1 = backward_layer(e1, layer1, saved1, geo, core, send_result, take_result)

    def take_late(kept):
        held["late"], kept = tie(late1, kept)
        return kept

    def take_early(dqkv):
        held["early"], dqkv = tie(early1, dqkv)
        return dqkv

    n_dp = lax.axis_size("dp")

    def small_sums(small0):
        mine = [choose(a, b) for a, b in zip(small0, small1)]
        theirs = [choose(b, a) for a, b in zip(small0, small1)]
        packed = lambda pair: jnp.concatenate([pair[0].reshape(-1), pair[1]])
        return butterfly(packed(mine) + swap(packed(theirs)), "dp")

    dx0, early0, late0, line = backward_layer(e0, layer0, saved0, geo, core, None, take_early, take_late, small_sums)

    y1, y1_got = held["y1"]
    boundary = jnp.stack([choose(dx0, y1_got), choose(to_first(dx0), y1)])[None]

    def halves(one, zero):
        from_first, from_second = to_next(one), to_first(zero)
        return choose(zero, from_first).astype(F32), choose(from_second, one).astype(F32)

    early, g_qkv = halves(held["early"], early0), halves(held["late"], late0)
    n_out, n_in = w_out.shape[1], w_in.shape[2]
    join = lambda f: jnp.concatenate([f(early[0]), f(early[1])], axis=0)
    g_out = join(lambda a: unpack_out(a[:, :n_out], n_out, d))
    g_in = join(lambda a: a[:, n_out:n_out + n_in])
    g_fc2 = join(lambda a: a[:, n_out + n_in:])
    g_qkv = jnp.concatenate(g_qkv, axis=0)

    at = 5 * d
    small, bias = line[:at].reshape(5, d), line[at:]
    small = butterfly(small, "tensor").reshape(small.shape[0], n_tensor * n_dp, -1)
    where = lax.axis_index("dp")
    pick = lambda a, i: lax.dynamic_index_in_dim(a, i, -2, keepdims=False)
    sums = pick(small, me * n_dp + where)
    n_qkv = b_qkv.size
    g_b_qkv = pick(column_order(bias[None, :n_qkv], -1).reshape(n_dp, -1), where)
    g_b_in = pick(bias[n_qkv:].reshape(n_dp, -1), where)
    g_gain, g_bias = sums[None, 0:2], sums[None, 2:4]
    g_out_bias = jnp.stack([sums[4], sums[4]])[None]
    return (
        boundary,
        g_gain,
        g_bias,
        column_order(g_qkv, -1)[None],
        g_b_qkv[None],
        g_out[None],
        g_in[None],
        g_b_in[None],
        g_fc2[None],
        g_out_bias,
    )


def solution(mesh):
    placed = (
        P("pipe", "dp", "tensor", None),
        P("dp", None),
        P("pipe", None, None),
        P("pipe", None, None),
        P("pipe", None, "tensor"),
        P("pipe", "tensor"),
        P("pipe", "tensor", None),
        P("pipe", None, "tensor"),
        P("pipe", "tensor"),
        P("pipe", "tensor", None),
        P("pipe", None, None),
    )
    return jax.shard_map(
        body,
        mesh=mesh,
        in_specs=placed,
        out_specs=(
            P("pipe", "dp", "tensor", None),
            P("pipe", None, ("tensor", "dp")),
            P("pipe", None, ("tensor", "dp")),
            P("pipe", "dp", "tensor"),
            P("pipe", ("tensor", "dp")),
            P("pipe", ("tensor", "dp"), None),
            P("pipe", "dp", "tensor"),
            P("pipe", ("tensor", "dp")),
            P("pipe", ("tensor", "dp"), None),
            P("pipe", None, ("tensor", "dp")),
        ),
        check_vma=False,
    )
```

```python
import functools
import math

import jax
import jax.numpy as jnp
from jax import lax
from jax.experimental import pallas as pl
from jax.experimental.pallas import tpu as pltpu
from jax.sharding import PartitionSpec as P

HEAD_DIM = 64
ROT = 16
EPSILON = 1e-05
MASKED = -1e30
TILE = 256
CHUNK = 512
SUB = 128
LANES = 128
BF = jnp.bfloat16
F32 = jnp.float32

VM = pltpu.VMEM
NT = (((1,), (1,)), ((), ()))
TN = (((0,), (0,)), ((), ()))


def dot_nn(a, b):
    return jnp.dot(a, b, preferred_element_type=F32)


def dot_nt(a, b):
    return lax.dot_general(a, b, NT, preferred_element_type=F32)


def dot_tn(a, b):
    return lax.dot_general(a, b, TN, preferred_element_type=F32)


def whole(shape):
    return pl.BlockSpec(shape, lambda *_: (0,) * len(shape))


SMEM_SPEC = pl.BlockSpec(memory_space=pltpu.SMEM)
ANY_SPEC = pl.BlockSpec(memory_space=pl.ANY)
PARAMS = pltpu.CompilerParams(vmem_limit_bytes=56 * 1024 * 1024)


def cost(flops, moved):
    return pl.CostEstimate(flops=int(flops), bytes_accessed=int(moved), transcendentals=0)


def norm_rows(rows):
    centre = jnp.mean(rows, axis=-1, keepdims=True)
    shifted = rows - centre
    inverse_std = lax.rsqrt(jnp.mean(shifted * shifted, axis=-1, keepdims=True) + EPSILON)
    return shifted * inverse_std, inverse_std


def turn(values, tables, direction):
    cos_t, sin_a, sin_b = tables
    width = values.shape[-1]
    times = width // LANES
    wide = lambda t: jnp.concatenate([t] * times, axis=1)
    ahead = pltpu.roll(values, width - ROT // 2, 1)
    behind = pltpu.roll(values, ROT // 2, 1)
    return values * wide(cos_t) + direction * (ahead * wide(sin_a) + behind * wide(sin_b))


SLOTS = (1, 2, 0, 3)
OWN, NEAR, FAR, ENDS = (1, 2), (2, 0), (1, 3), (2, 1)


def stacked(refs):
    parts = [r[...] for r in refs]
    return parts[0] if len(parts) == 1 else jnp.concatenate(parts, axis=0)


def pre_kernel(n_x, n_alias, *refs):
    x_refs = refs[:n_x]
    (gain_ref, bias_ref, wqkv_ref, bqkv_ref, win_ref, bin_ref, cos_ref, sa_ref, sb_ref) = refs[n_x:n_x + 9]
    n1_ref, n2_ref, q_ref, k_ref, v_ref, g_ref, slope_ref, n2_keep = refs[n_x + 9 + n_alias:]

    @pl.when(pl.program_id(0) == 0)
    def _():
        normal, _ = norm_rows(stacked(x_refs).astype(F32))
        gains = gain_ref[...].astype(F32)
        biases = bias_ref[...].astype(F32)
        n1 = (normal * gains[0:1] + biases[0:1]).astype(BF)
        n2 = (normal * gains[1:2] + biases[1:2]).astype(BF)
        n1_ref[...] = n1.reshape(n1_ref.shape)
        n2_ref[...] = n2.reshape(n2_ref.shape)
        n2_keep[...] = n2
        flat = lambda r: r[...].reshape(n1.shape[0], LANES)
        tables = (flat(cos_ref), flat(sa_ref), flat(sb_ref))
        wide = q_ref.shape[-1]
        scale = 1.0 / math.sqrt(HEAD_DIM)
        bq = bqkv_ref[...].astype(F32)
        part = lambda i: dot_nn(n1, wqkv_ref[:, i * wide:(i + 1) * wide]) + bq[:, i * wide:(i + 1) * wide]
        q = (turn(part(0), tables, 1.0).astype(BF).astype(F32) * scale).astype(BF)
        q_ref[...] = q.reshape(q_ref.shape)
        k_ref[...] = turn(part(1), tables, 1.0).astype(BF).reshape(k_ref.shape)
        v_ref[...] = part(2).astype(BF).reshape(v_ref.shape)

    f = dot_nn(n2_keep[...], win_ref[...]) + bin_ref[...].astype(F32)
    phi = 0.5 * (1.0 + lax.erf(f * (1.0 / math.sqrt(2.0))))
    density = jnp.exp(-0.5 * f * f) * (1.0 / math.sqrt(2.0 * math.pi))
    g_ref[...] = (f * phi).astype(BF).reshape(g_ref.shape)
    slope_ref[...] = (phi + f * density).astype(BF).reshape(slope_ref.shape)


def group_call(kernel, args, in_specs, outs, kept, grid, scratch, price):
    n_alias = 0 if kept is None else len(outs)
    specs = list(in_specs)
    operands = list(args)
    aliases = {}
    if kept is not None:
        for i, buf in enumerate(kept):
            aliases[len(operands)] = i
            operands.append(buf)
            specs.append(ANY_SPEC)
    return pl.pallas_call(
        functools.partial(kernel, n_alias),
        grid=grid,
        in_specs=specs,
        out_specs=[pl.BlockSpec(block, index) for _, _, block, index in outs],
        out_shape=[jax.ShapeDtypeStruct(shape, dtype) for shape, dtype, _, _ in outs],
        input_output_aliases=aliases,
        scratch_shapes=scratch,
        compiler_params=PARAMS,
        cost_estimate=price,
    )(*operands)


def pre_group(group, xs, lp, tables, kept):
    size, at = group
    d = xs[0].shape[1]
    slots, rows = len(SLOTS), tables[0].shape[1]
    total = size * rows
    wide = lp["w_qkv"].shape[1]
    units = lp["w_in"].shape[1]
    cols = wide // 3
    ck = min(CHUNK, units)
    first = lambda j: (at, 0, 0)
    moving = lambda j: (at, 0, j)
    outs = [((slots, rows, d), BF, (size, rows, d), first)] * 2
    outs += [((slots, rows, cols), BF, (size, rows, cols), first)] * 3
    outs += [((slots, rows, units), BF, (size, rows, ck), moving)] * 2
    in_specs = [whole(x.shape) for x in xs]
    in_specs += [whole((2, d)), whole((2, d)), whole((d, wide)), whole((1, wide)),
                 pl.BlockSpec((d, ck), lambda j: (0, j)), pl.BlockSpec((1, ck), lambda j: (0, j))]
    in_specs += [pl.BlockSpec((size, rows, LANES), first)] * 3
    args = [*xs, lp["ln_gain"], lp["ln_bias"], lp["w_qkv"], lp["b_qkv"], lp["w_in"], lp["b_in"], *tables]
    return group_call(functools.partial(pre_kernel, len(xs)), args, in_specs, outs, kept, (units // ck,),
                      [VM((total, d), BF)],
                      cost(2 * total * d * (wide + units), 2 * d * (wide + units) + 10 * total * d))


def share(part, addend_refs, outs):
    if len(outs) == 3:
        own, far_a, far_b = outs
        rows, half = own.shape[0], far_a.shape[0]
        own[...] = part[:rows]
        far_a[...] = part[rows:rows + half].astype(BF)
        far_b[...] = part[rows + half:].astype(BF)
        return
    one, two = outs
    from_two, from_one = addend_refs
    rows, half = one.shape[0], from_two.shape[0]
    one[:half, :] = part[:half].astype(BF)
    one[half:, :] = (part[half:rows] + from_two[...].astype(F32)).astype(BF)
    two[:half, :] = (part[rows:rows + half] + from_one[...].astype(F32)).astype(BF)
    two[half:, :] = part[rows + half:].astype(BF)


def share_specs(group, rows, d, ck):
    col = lambda j: (0, j)
    if group == ENDS:
        shapes = [((rows, d), F32), ((rows // 2, d), BF), ((rows // 2, d), BF)]
    else:
        shapes = [((rows, d), BF), ((rows, d), BF)]
    return [pl.BlockSpec((s[0], ck), col) for s, _ in shapes], [jax.ShapeDtypeStruct(s, t) for s, t in shapes]


def post_kernel(n_add, o_ref, g_ref, wout_ref, wfc_ref, *rest):
    total = o_ref.shape[0] * o_ref.shape[1]
    o = o_ref[...].reshape(total, o_ref.shape[-1])
    g = g_ref[...].reshape(total, g_ref.shape[-1])
    share(dot_nn(o, wout_ref[...]) + dot_nn(g, wfc_ref[...]), rest[:n_add], rest[n_add:])


def post_group(group, o_all, g_all, lp, addends):
    size, at = group
    _, rows, cols = o_all.shape
    units, d = lp["w_fc2"].shape
    ck = min(CHUNK, d)
    fixed = lambda j: (at, 0, 0)
    in_specs = [pl.BlockSpec((size, rows, cols), fixed), pl.BlockSpec((size, rows, units), fixed),
                pl.BlockSpec((cols, ck), lambda j: (0, j)), pl.BlockSpec((units, ck), lambda j: (0, j))]
    in_specs += [pl.BlockSpec((a.shape[0], ck), lambda j: (0, j)) for a in addends]
    out_specs, out_shape = share_specs(group, rows, d, ck)
    total = size * rows
    return pl.pallas_call(
        functools.partial(post_kernel, len(addends)),
        grid=(d // ck,),
        in_specs=in_specs,
        out_specs=out_specs,
        out_shape=out_shape,
        compiler_params=PARAMS,
        cost_estimate=cost(2 * total * d * (cols + units), 2 * d * (cols + units) + 5 * total * d),
    )(o_all, g_all, lp["w_out"], lp["w_fc2"], *addends)


def bpre_kernel(n_x, n_alias, *refs):
    e_refs = refs[:n_x]
    wout_ref, wfc_ref, slope_ref = refs[n_x:n_x + 3]
    eall_ref, do_ref, df_ref, sums_ref = refs[n_x + 3 + n_alias:]
    e = stacked(e_refs)

    @pl.when(pl.program_id(0) == 0)
    def _():
        eall_ref[...] = e.reshape(eall_ref.shape)
        do_ref[...] = dot_nt(e, wout_ref[...]).astype(BF).reshape(do_ref.shape)

    back = dot_nt(e, wfc_ref[...])
    df = (back * slope_ref[...].reshape(back.shape).astype(F32)).astype(BF)
    df_ref[...] = df.reshape(df_ref.shape)
    sums = jnp.sum(df.astype(F32).reshape(df_ref.shape), axis=1, keepdims=True)
    sums_ref[...] = sums


def bpre_group(group, es, slope_all, lp, kept):
    size, at = group
    d = es[0].shape[1]
    slots, rows, units = slope_all.shape
    cols = lp["w_out"].shape[0]
    ck = min(CHUNK, units)
    first = lambda j: (at, 0, 0)
    moving = lambda j: (at, 0, j)
    outs = [((slots, rows, d), BF, (size, rows, d), first), ((slots, rows, cols), BF, (size, rows, cols), first),
            ((slots, rows, units), BF, (size, rows, ck), moving), ((slots, 1, units), F32, (size, 1, ck), moving)]
    in_specs = [whole(e.shape) for e in es]
    in_specs += [whole((cols, d)), pl.BlockSpec((ck, d), lambda j: (j, 0)),
                 pl.BlockSpec((size, rows, ck), moving)]
    args = [*es, lp["w_out"], lp["w_fc2"], slope_all]
    total = size * rows
    return group_call(functools.partial(bpre_kernel, len(es)), args, in_specs, outs, kept, (units // ck,), [],
                      cost(2 * total * d * (cols + units), 2 * d * (cols + units) + 8 * total * d))


def bpost_kernel(n_x, n_add, ck, *refs):
    x_refs = refs[:n_x]
    gain_ref, dqkv_ref, df_ref, wqkv_ref, win_ref = refs[n_x:n_x + 5]
    addend_refs = refs[n_x + 5:n_x + 5 + n_add]
    outs = refs[n_x + 5 + n_add:-2]
    sums_ref, normal_keep = refs[-2:]
    j = pl.program_id(0)

    @pl.when(j == 0)
    def _():
        normal, _ = norm_rows(stacked(x_refs).astype(F32))
        for c in range(normal_keep.shape[0]):
            normal_keep[c] = normal[:, c * ck:(c + 1) * ck]

    normal = normal_keep[j]
    flat = lambda r: r[...].reshape(normal.shape[0], r.shape[-1])
    one = dot_nt(flat(dqkv_ref), wqkv_ref[...])
    two = dot_nt(flat(df_ref), win_ref[...])
    total = lambda v: jnp.sum(v, axis=0, keepdims=True)
    sums_ref[0:1, :] = total(one * normal)
    sums_ref[1:2, :] = total(two * normal)
    sums_ref[2:3, :] = total(one)
    sums_ref[3:4, :] = total(two)
    gains = gain_ref[...].astype(F32)
    share(one * gains[0:1] + two * gains[1:2], addend_refs, outs)


def bpost_group(group, xs, dqkv_all, df_all, lp, addends):
    size, at = group
    d = xs[0].shape[1]
    _, rows, wide = dqkv_all.shape
    units = df_all.shape[-1]
    ck = min(CHUNK, d)
    total = size * rows
    fixed = lambda j: (at, 0, 0)
    in_specs = [whole(x.shape) for x in xs]
    in_specs += [pl.BlockSpec((2, ck), lambda j: (0, j)),
                 pl.BlockSpec((size, rows, wide), fixed), pl.BlockSpec((size, rows, units), fixed),
                 pl.BlockSpec((ck, wide), lambda j: (j, 0)), pl.BlockSpec((ck, units), lambda j: (j, 0))]
    in_specs += [pl.BlockSpec((a.shape[0], ck), lambda j: (0, j)) for a in addends]
    out_specs, out_shape = share_specs(group, rows, d, ck)
    return pl.pallas_call(
        functools.partial(bpost_kernel, len(xs), len(addends), ck),
        grid=(d // ck,),
        in_specs=in_specs,
        out_specs=out_specs + [pl.BlockSpec((4, ck), lambda j: (0, j))],
        out_shape=out_shape + [jax.ShapeDtypeStruct((4, d), F32)],
        scratch_shapes=[VM((d // ck, total, ck), F32)],
        compiler_params=PARAMS,
        cost_estimate=cost(2 * total * d * (wide + units), 2 * d * (wide + units) + 7 * total * d),
    )(*xs, lp["ln_gain"], dqkv_all, df_all, lp["w_qkv"], lp["w_in"], *addends)


def wgrad_kernel(with_out, core_ref, *refs):
    first = core_ref[0] == 0
    if with_out:
        keep_ref, give_ref, whole_out = refs[-3:]
        pairs = list(refs[2:-3])
    else:
        keep_ref, give_ref = refs[-2:]
        pairs = list(refs[:-2])
    many, half, _ = keep_ref.shape

    def store(b, rows, cols, zero, one):
        keep_ref[b, rows, cols] = jnp.where(first, zero, one).astype(BF)
        give_ref[b, rows, cols] = jnp.where(first, one, zero).astype(BF)

    at = 0
    if with_out:
        o_ref, e_ref = refs[:2]
        cols = o_ref.shape[1]
        j = pl.program_id(0)

        @pl.when(j == 0)
        def _():
            whole_out[...] = dot_tn(o_ref[...], e_ref[...])

        groups = e_ref.shape[1] // cols
        few = half // groups
        for b in range(many):
            start = 2 * (j * many + b)
            zero, one = [whole_out[pl.ds(pl.multiple_of((start + h) * few, few), few), :] for h in range(2)]
            for c in range(groups):
                part = slice(c * cols, (c + 1) * cols)
                store(b, slice(c * few, (c + 1) * few), slice(0, cols), zero[:, part], one[:, part])
        at = cols
        pairs.append(e_ref)
    for a_ref, b_ref in zip(pairs[0::2], pairs[1::2]):
        wide = b_ref.shape[1]
        product = dot_tn(a_ref[...], b_ref[...])
        for b in range(many):
            low = 2 * b * half
            store(b, slice(None), slice(at, at + wide), product[low:low + half], product[low + half:low + 2 * half])
        at += wide


def wgrad_shapes(d, cols):
    n = lax.axis_size("dp")
    block = d // n
    lanes = max(block, LANES)
    many = lanes // block
    specs = [pl.BlockSpec((many, block // 2, cols), lambda j: (j, 0, 0))] * 2
    shapes = [jax.ShapeDtypeStruct((n, block // 2, cols), BF)] * 2
    return d // lanes, lanes, specs, shapes


def wgrad_early(core, o, e, n2, df, g):
    length, d = e.shape
    cols = o.shape[1] + df.shape[1] + d
    steps, lanes, specs, shapes = wgrad_shapes(d, cols)
    moving = pl.BlockSpec((length, lanes), lambda j: (0, j))
    return pl.pallas_call(
        functools.partial(wgrad_kernel, True),
        grid=(steps,),
        in_specs=[SMEM_SPEC, whole(o.shape), whole(e.shape), moving, whole(df.shape), moving],
        out_specs=specs,
        out_shape=shapes,
        scratch_shapes=[VM((o.shape[1], d), F32)],
        compiler_params=PARAMS,
        cost_estimate=cost(2 * length * d * cols, 2 * length * 4 * d + 2 * d * cols),
    )(core, o, e, n2, df, g)


def wgrad_late(core, n1, dqkv):
    length, d = n1.shape
    cols = dqkv.shape[1]
    steps, lanes, specs, shapes = wgrad_shapes(d, cols)
    return pl.pallas_call(
        functools.partial(wgrad_kernel, False),
        grid=(steps,),
        in_specs=[SMEM_SPEC, pl.BlockSpec((length, lanes), lambda j: (0, j)), whole(dqkv.shape)],
        out_specs=specs,
        out_shape=shapes,
        compiler_params=PARAMS,
        cost_estimate=cost(2 * length * d * cols, 2 * length * 2 * d + 2 * d * cols),
    )(core, n1, dqkv)


def head_lanes(shape):
    return lax.broadcasted_iota(jnp.int32, shape, len(shape) - 1) // HEAD_DIM


def attend_kernel(order_ref, low_ref, q_ref, k_ref, v_ref, start_ref, o_ref, lse_ref,
                  k_abs, v_turned, acc, qm, top, tot):
    subs, _, cols = q_ref.shape
    heads = cols // HEAD_DIM
    per = TILE // SUB
    blocks = subs // per
    for b in range(blocks):
        pair = [order_ref[b * per + u] for u in range(per)]
        k_abs[b * TILE:(b + 1) * TILE, :] = jnp.concatenate([k_ref[s] for s in pair], axis=0)
        v_turned[b] = jnp.transpose(jnp.concatenate([v_ref[s] for s in pair], axis=0))

    def one_query(qb, _):
        srcs = [order_ref[qb * per + u] for u in range(per)]
        q = jnp.concatenate([q_ref[s] for s in srcs], axis=0)
        base = qb * TILE
        starts = start_ref[qb]
        places = base + lax.broadcasted_iota(jnp.int32, (1, TILE), 1)
        group = head_lanes(q.shape)
        for h in range(heads):
            qm[h] = jnp.where(group == h, q, jnp.zeros_like(q))
        down = lax.broadcasted_iota(jnp.int32, (TILE, TILE), 0)

        def scores(kb):
            at = pl.multiple_of(kb * TILE, TILE)
            keys = k_abs[pl.ds(at, TILE), :]
            allowed = jnp.logical_and(down + at >= starts, down + at <= places)
            return [jnp.where(allowed, dot_nt(keys, qm[h]), MASKED) for h in range(heads)]

        found = scores(qb)
        for h in range(heads):
            lanes = slice(h * HEAD_DIM, (h + 1) * HEAD_DIM)
            m = jnp.max(found[h], axis=0, keepdims=True)
            p = jnp.exp(found[h] - m)
            top[h] = m
            tot[h] = jnp.sum(p, axis=0, keepdims=True)
            acc[lanes, :] = dot_nn(v_turned[qb, lanes, :], p.astype(BF))

        def one_key(kb, _):
            found = scores(kb)
            for h in range(heads):
                lanes = slice(h * HEAD_DIM, (h + 1) * HEAD_DIM)
                old = top[h]
                m = jnp.maximum(old, jnp.max(found[h], axis=0, keepdims=True))
                fade = jnp.exp(old - m)
                p = jnp.exp(found[h] - m)
                top[h] = m
                tot[h] = tot[h] * fade + jnp.sum(p, axis=0, keepdims=True)
                acc[lanes, :] = acc[lanes, :] * fade + dot_nn(v_turned[kb, lanes, :], p.astype(BF))
            return 0

        lax.fori_loop(low_ref[qb], qb, one_key, 0)
        for h in range(heads):
            lanes = slice(h * HEAD_DIM, (h + 1) * HEAD_DIM)
            acc[lanes, :] = acc[lanes, :] / tot[h]
            lse_ref[qb, h:h + 1, :] = top[h] + jnp.log(tot[h])
        out = jnp.transpose(acc[...]).astype(BF)
        for u in range(per):
            o_ref[srcs[u]] = out[u * SUB:(u + 1) * SUB]
        return 0

    lax.fori_loop(0, blocks, one_query, 0)


def attend(order, low, q, k, v, start_rows):
    subs, _, cols = q.shape
    length = subs * SUB
    heads = cols // HEAD_DIM
    blocks = length // TILE
    full = [whole(a.shape) for a in (q, k, v, start_rows)]
    return pl.pallas_call(
        attend_kernel,
        grid=(1,),
        in_specs=[SMEM_SPEC, SMEM_SPEC] + full,
        out_specs=[whole(q.shape), whole((blocks, 8, TILE))],
        out_shape=[jax.ShapeDtypeStruct(q.shape, BF), jax.ShapeDtypeStruct((blocks, 8, TILE), F32)],
        scratch_shapes=[VM((length, cols), BF), VM((blocks, cols, TILE), BF), VM((cols, TILE), F32),
                        VM((heads, TILE, cols), BF), VM((heads, 1, TILE), F32), VM((heads, 1, TILE), F32)],
        compiler_params=PARAMS,
        cost_estimate=cost(3 * length * length * cols, 5 * length * cols),
    )(order, low, q, k, v, start_rows)


def attend_back_kernel(order_ref, low_ref, q_ref, k_ref, v_ref, do_ref, o_ref, lse_ref, start_ref,
                       cos_ref, sa_ref, sb_ref, out_ref, sums_ref,
                       k_abs, v_abs, km, dk, dv, dq, qm, dom, stat):
    subs, _, cols = q_ref.shape
    heads = cols // HEAD_DIM
    per = TILE // SUB
    scale = 1.0 / math.sqrt(HEAD_DIM)
    for i in range(subs):
        src = order_ref[i]
        rows = slice(i * SUB, (i + 1) * SUB)
        key = k_ref[src]
        k_abs[rows, :] = key
        v_abs[rows, :] = v_ref[src]
        for h in range(heads):
            km[h, rows, :] = jnp.where(head_lanes(key.shape) == h, key, jnp.zeros_like(key))
        dk[rows, :] = jnp.zeros((SUB, cols), F32)
        dv[rows, :] = jnp.zeros((SUB, cols), F32)
    sums_ref[...] = jnp.zeros(sums_ref.shape, F32)

    def tables(src):
        return cos_ref[src], sa_ref[src], sb_ref[src]

    def emit(src, at, values):
        low = values.astype(BF)
        out_ref[src, :, at:at + cols] = low
        sums_ref[:, at:at + cols] += jnp.sum(low.astype(F32), axis=0, keepdims=True)

    def one_query(qb, _):
        base = pl.multiple_of(qb * TILE, TILE)
        srcs = [order_ref[qb * per + u] for u in range(per)]
        q = jnp.concatenate([q_ref[s] for s in srcs], axis=0)
        do = jnp.concatenate([do_ref[s] for s in srcs], axis=0)
        o = jnp.concatenate([o_ref[s] for s in srcs], axis=0)
        group = head_lanes(q.shape)
        logs = lse_ref[qb]
        inner = jnp.transpose(do.astype(F32) * o.astype(F32))
        for h in range(heads):
            qm[h] = jnp.where(group == h, q, jnp.zeros_like(q))
            dom[h] = jnp.where(group == h, do, jnp.zeros_like(do))
            stat[h, 0:1, :] = logs[h:h + 1, :]
            stat[h, 1:2, :] = jnp.sum(inner[h * HEAD_DIM:(h + 1) * HEAD_DIM, :], axis=0, keepdims=True)
        dq[...] = jnp.zeros((TILE, cols), F32)
        starts = start_ref[qb]
        places = base + lax.broadcasted_iota(jnp.int32, (1, TILE), 1)
        down = lax.broadcasted_iota(jnp.int32, (TILE, TILE), 0)

        def one_key(kb, _):
            at = pl.multiple_of(kb * TILE, TILE)
            keys = k_abs[pl.ds(at, TILE), :]
            vals = v_abs[pl.ds(at, TILE), :]
            allowed = jnp.logical_and(down + at >= starts, down + at <= places)
            dk_new = dv_new = dq_new = None
            more = lambda old, new: new if old is None else old + new
            for h in range(heads):
                s = dot_nt(keys, qm[h])
                p = jnp.exp(jnp.where(allowed, s - stat[h, 0:1, :], MASKED))
                dp = dot_nt(vals, dom[h])
                ds = (p * (dp - stat[h, 1:2, :])).astype(BF)
                dv_new = more(dv_new, dot_nn(p.astype(BF), dom[h]))
                dk_new = more(dk_new, dot_nn(ds, qm[h]))
                dq_new = more(dq_new, dot_tn(ds, km[h, pl.ds(at, TILE), :]))
            dv[pl.ds(at, TILE), :] += dv_new
            dk[pl.ds(at, TILE), :] += dk_new
            dq[...] += dq_new
            return 0

        lax.fori_loop(low_ref[qb], qb + 1, one_key, 0)
        for u in range(per):
            emit(srcs[u], 0, turn(dq[u * SUB:(u + 1) * SUB, :] * scale, tables(srcs[u]), -1.0))
        return 0

    lax.fori_loop(0, subs // per, one_query, 0)
    for i in range(subs):
        src = order_ref[i]
        rows = slice(i * SUB, (i + 1) * SUB)
        emit(src, cols, turn(dk[rows, :], tables(src), -1.0))
        emit(src, 2 * cols, dv[rows, :])


def attend_back(order, low, q, k, v, do, o, lse, start_rows, tables):
    subs, _, cols = q.shape
    length = subs * SUB
    heads = cols // HEAD_DIM
    args = (q, k, v, do, o, lse, start_rows, *tables)
    return pl.pallas_call(
        attend_back_kernel,
        grid=(1,),
        in_specs=[SMEM_SPEC, SMEM_SPEC] + [whole(a.shape) for a in args],
        out_specs=[whole((subs, SUB, 3 * cols)), whole((1, 3 * cols))],
        out_shape=[jax.ShapeDtypeStruct((subs, SUB, 3 * cols), BF), jax.ShapeDtypeStruct((1, 3 * cols), F32)],
        scratch_shapes=[VM((length, cols), BF), VM((length, cols), BF), VM((heads, length, cols), BF),
                        VM((length, cols), F32), VM((length, cols), F32), VM((TILE, cols), F32),
                        VM((heads, TILE, cols), BF), VM((heads, TILE, cols), BF), VM((heads, 2, TILE), F32)],
        compiler_params=PARAMS,
        cost_estimate=cost(8 * length * length * cols, 16 * length * cols),
    )(order, low, *args)


def across(x, k):
    n = lax.axis_size("tensor")
    return lax.ppermute(x, "tensor", [(i, i ^ k) for i in range(n)])


def swap(x):
    return lax.ppermute(x, "pipe", [(0, 1), (1, 0)])


def gather_and_run(x, call, beside=None, near=None):
    half = x.shape[0] // 2
    one, two = across(x, 1), across(x, 2)
    kept = call(OWN, [x], None)
    one, two, kept = lax.optimization_barrier((one, two, kept))
    far_a = across(one[:half], 2)
    far_b = across(two[half:], 1)
    kept = call(NEAR, [one, two], kept)
    if near is not None:
        kept = near(kept)
    far_a, far_b, kept, beside = lax.optimization_barrier((far_a, far_b, kept, beside))
    kept = call(FAR, [far_a, far_b], kept)
    return (x, one, two, far_a, far_b), kept, beside


def add_rows(own, got_one, got_two):
    return own + got_one.astype(F32) + got_two.astype(F32)


def dp_reduce(blocks):
    n, rows, cols = blocks.shape
    return lax.psum_scatter(blocks.reshape(n * rows, cols), "dp", scatter_dimension=0, tiled=True)


def butterfly(vec, axis):
    n = lax.axis_size(axis)
    k = 1
    while k < n:
        vec = vec + lax.ppermute(vec, axis, [(i, i ^ k) for i in range(n)])
        k *= 2
    return vec


def flat(a):
    return a.reshape(-1, SUB, a.shape[-1])


NAMES = ("w_qkv", "w_out", "w_in", "w_fc2")


def rows2(a):
    return a.reshape(-1, a.shape[-1])


def tie(*values):
    return lax.optimization_barrier(values)


def forward_layer(x, lp, geo, beside=None):
    call = lambda group, xs, kept: pre_group(group, xs, lp, geo["tables"], kept)
    rows, kept, beside = gather_and_run(x, call, beside)
    n1, n2, q, k, v, g, slope = kept
    o, lse = attend(geo["order"], geo["low"], flat(q), flat(k), flat(v), geo["start_rows"])
    saved = dict(rows=rows, n1=n1, n2=n2, q=flat(q), k=flat(k), v=flat(v), g=g, slope=slope, o=o, lse=lse)
    return saved, beside


def branches(saved, lp):
    g = saved["g"]
    o_slots = saved["o"].reshape(*g.shape[:2], -1)
    own, far_a, far_b = post_group(ENDS, o_slots, g, lp, [])
    from_one, from_two = across(far_a, 1), across(far_b, 2)
    one, two = post_group(NEAR, o_slots, g, lp, [from_two, from_one])
    return own, one, two


def layer_result(saved, lp, own, got_one, got_two):
    out_biases = lp["out_bias"].astype(F32)
    summed = add_rows(own, got_one, got_two)
    return (saved["rows"][0].astype(F32) + summed + out_biases[0] + out_biases[1]).astype(BF)


def over_chip(pair):
    return (pair[0].astype(F32) + swap(pair[1]).astype(F32)).astype(BF)


def input_grad(e, x, u):
    x_rows, e_rows = x.astype(F32), e.astype(F32)
    normal, inverse_std = norm_rows(x_rows)
    mean_grad = jnp.mean(u, axis=-1, keepdims=True)
    mean_cross = jnp.mean(u * normal, axis=-1, keepdims=True)
    return (e_rows + (u - mean_grad - normal * mean_cross) * inverse_std).astype(BF)


def back_attention(saved, do, geo):
    return attend_back(geo["order"], geo["low"], saved["q"], saved["k"], saved["v"], flat(do),
                       saved["o"], saved["lse"], geo["start_rows"], geo["flat_tables"])


def backward_layer(e, lp, saved, geo, core, before=None, after=None, near=None, ending=None):
    last = ending is not None
    call = lambda group, es, kept: bpre_group(group, es, saved["slope"], lp, kept)
    _, kept, _ = gather_and_run(e, call, near=near)
    e_all, do, df, bin_parts = kept
    early = wgrad_early(core, rows2(saved["o"]), rows2(e_all), rows2(saved["n2"]), rows2(df), rows2(saved["g"]))
    if before is not None:
        do = before(do)
    if last:
        early, do = tie(over_chip(early), do)
        early = dp_reduce(early)
    dqkv, bqkv_grad = back_attention(saved, do, geo)
    if after is not None:
        dqkv = after(dqkv)
    x, x_one, x_two, x_far_a, x_far_b = saved["rows"]
    dqkv_slots = dqkv.reshape(*df.shape[:2], dqkv.shape[-1])
    own, far_a, far_b, sums_a = bpost_group(ENDS, [x, x_far_a, x_far_b], dqkv_slots, df, lp, [])
    far_a, far_b, dqkv = tie(far_a, far_b, dqkv)
    from_one, from_two = across(far_a, 1), across(far_b, 2)
    late = wgrad_late(core, rows2(saved["n1"]), rows2(dqkv))
    if last:
        late = over_chip(late)
    late, from_one, from_two = tie(late, from_one, from_two)
    one, two, sums_b = bpost_group(NEAR, [x_one, x_two], dqkv_slots, df, lp, [from_two, from_one])
    got_one, got_two = across(one, 1), across(two, 2)
    small = jnp.concatenate([sums_a + sums_b, jnp.sum(e.astype(F32), axis=0, keepdims=True)], axis=0)
    bias_grads = jnp.concatenate([bqkv_grad[0], jnp.sum(bin_parts, axis=(0, 1))])
    small = (small, bias_grads)
    if last:
        early, late = tie(early, late)
        small = ending(small)
        small, got_one, got_two = tie(small, got_one, got_two)
        late = dp_reduce(late)
    else:
        late = dp_reduce(over_chip(late))
        early, got_one, got_two = tie(early, got_one, got_two)
        early = dp_reduce(over_chip(early))
    dx = input_grad(e, x, add_rows(own, got_one, got_two))
    if last:
        late, dx = tie(late, dx)
    return dx, early, late, small


def unpack_out(g, rows, d):
    groups = d // rows
    return jnp.swapaxes(g.reshape(groups, -1, rows), 0, 1).reshape(-1, d)


def column_order(a, direction):
    shape = a.shape
    heads = shape[-1] // (3 * HEAD_DIM)
    dims = (heads, 3) if direction > 0 else (3, heads)
    split = a.reshape(*shape[:-1], *dims, HEAD_DIM)
    return jnp.swapaxes(split, -2, -3).reshape(shape)


def body(ends, segments, ln_gain, ln_bias, w_qkv, b_qkv, w_out, w_in, b_in, w_fc2, out_bias):
    is_first = lax.axis_index("pipe") == 0
    me = lax.axis_index("tensor")
    n_tensor = lax.axis_size("tensor")
    choose = lambda a, b: jnp.where(is_first, a, b)
    shares = ends[0]
    rows, d = shares.shape[1:]

    got = swap(shares)
    x0 = choose(shares[0], got[1])
    e1 = choose(got[0], shares[1])

    own = dict(ln_gain=ln_gain[0], ln_bias=ln_bias[0], w_qkv=column_order(w_qkv[0], 1),
               b_qkv=column_order(b_qkv, 1), w_out=w_out[0], w_in=w_in[0], b_in=b_in, w_fc2=w_fc2[0],
               out_bias=out_bias[0])
    own, x0, e1 = tie(own, x0, e1)
    small_names = ("ln_gain", "ln_bias", "b_qkv", "b_in", "out_bias")
    packed = jnp.concatenate([own[s].reshape(-1) for s in small_names]).reshape(-1, LANES)
    other_packed = swap(packed).reshape(-1)
    other = {name: swap(own[name]) for name in NAMES}
    at = 0
    for s in small_names:
        other[s] = other_packed[at:at + own[s].size].reshape(own[s].shape)
        at += own[s].size
    layer0 = {name: choose(own[name], other[name]) for name in own}
    layer1 = {name: choose(other[name], own[name]) for name in own}

    segment_row = choose(segments[0], segments[1])
    length = segment_row.shape[0]
    places = jnp.arange(length, dtype=jnp.int32)
    begins = jnp.concatenate([jnp.ones((1,), dtype=jnp.bool_), segment_row[1:] != segment_row[:-1]])
    starts = lax.cummax(jnp.where(begins, places, 0), axis=0)
    slot_index = jnp.array(SLOTS, dtype=jnp.int32) ^ me
    by_slot = jnp.take((places - starts).reshape(n_tensor, rows), slot_index, axis=0)
    x0, by_slot = lax.optimization_barrier((x0, by_slot))
    lane = jnp.arange(LANES, dtype=jnp.int32) % HEAD_DIM
    half_rot = ROT // 2
    frequency = jnp.power(10000.0, -2.0 * (lane % half_rot).astype(F32) / ROT)
    angles = by_slot.astype(F32)[:, :, None] * frequency
    sines = jnp.sin(angles)
    tables = (jnp.where(lane < ROT, jnp.cos(angles), 1.0),
              jnp.where(lane < half_rot, -sines, 0.0),
              jnp.where(jnp.logical_and(lane >= half_rot, lane < ROT), sines, 0.0))
    per = rows // SUB
    subs = jnp.arange(length // SUB, dtype=jnp.int32)
    place_of = jnp.array([SLOTS.index(k) for k in range(n_tensor)], dtype=jnp.int32)
    tables = lax.optimization_barrier(tables)
    geo = dict(
        tables=tables,
        flat_tables=[flat(t) for t in tables],
        order=(place_of[(subs // per) ^ me] * per + subs % per).astype(jnp.int32),
        low=(starts.reshape(-1, TILE)[:, 0] // TILE).astype(jnp.int32),
        start_rows=starts.reshape(-1, 1, TILE),
    )

    core = lax.axis_index("pipe").astype(jnp.int32).reshape(1)
    saved0, _ = forward_layer(x0, layer0, geo)
    own, one, two = branches(saved0, layer0)
    h = layer_result(saved0, layer0, own, across(one, 1), across(two, 2))
    saved1, e1 = forward_layer(h, layer1, geo, e1)

    to_next = lambda a: lax.ppermute(a, "pipe", [(0, 1)])
    to_first = lambda a: lax.ppermute(a, "pipe", [(1, 0)])
    held = {}

    def send_result(do):
        own, one, two = branches(saved1, layer1)
        one, two, do = tie(one, two, do)
        held["y"] = own, across(one, 1), across(two, 2)
        return do

    def take_result(dqkv):
        own, got_one, got_two = held["y"]
        got_one, got_two, dqkv = tie(got_one, got_two, dqkv)
        y1 = layer_result(saved1, layer1, own, got_one, got_two)
        held["y1"] = y1, to_next(y1)
        return dqkv

    e0, early1, late1, small1 = backward_layer(e1, layer1, saved1, geo, core, send_result, take_result)

    def take_late(kept):
        held["late"], kept = tie(late1, kept)
        return kept

    def take_early(dqkv):
        held["early"], dqkv = tie(early1, dqkv)
        return dqkv

    n_dp = lax.axis_size("dp")

    def small_sums(small0):
        mine = [choose(a, b) for a, b in zip(small0, small1)]
        theirs = [choose(b, a) for a, b in zip(small0, small1)]
        packed = lambda pair: jnp.concatenate([pair[0].reshape(-1), pair[1]])
        return butterfly(packed(mine) + swap(packed(theirs)), "dp")

    dx0, early0, late0, line = backward_layer(e0, layer0, saved0, geo, core, None, take_early, take_late, small_sums)

    y1, y1_got = held["y1"]
    boundary = jnp.stack([choose(dx0, y1_got), choose(to_first(dx0), y1)])[None]

    def halves(one, zero):
        from_first, from_second = to_next(one), to_first(zero)
        return choose(zero, from_first).astype(F32), choose(from_second, one).astype(F32)

    early, g_qkv = halves(held["early"], early0), halves(held["late"], late0)
    n_out, n_in = w_out.shape[1], w_in.shape[2]
    join = lambda f: jnp.concatenate([f(early[0]), f(early[1])], axis=0)
    g_out = join(lambda a: unpack_out(a[:, :n_out], n_out, d))
    g_in = join(lambda a: a[:, n_out:n_out + n_in])
    g_fc2 = join(lambda a: a[:, n_out + n_in:])
    g_qkv = jnp.concatenate(g_qkv, axis=0)

    at = 5 * d
    small, bias = line[:at].reshape(5, d), line[at:]
    small = butterfly(small, "tensor").reshape(small.shape[0], n_tensor * n_dp, -1)
    where = lax.axis_index("dp")
    pick = lambda a, i: lax.dynamic_index_in_dim(a, i, -2, keepdims=False)
    sums = pick(small, me * n_dp + where)
    n_qkv = b_qkv.size
    g_b_qkv = pick(column_order(bias[None, :n_qkv], -1).reshape(n_dp, -1), where)
    g_b_in = pick(bias[n_qkv:].reshape(n_dp, -1), where)
    g_gain, g_bias = sums[None, 0:2], sums[None, 2:4]
    g_out_bias = jnp.stack([sums[4], sums[4]])[None]
    return (
        boundary,
        g_gain,
        g_bias,
        column_order(g_qkv, -1)[None],
        g_b_qkv[None],
        g_out[None],
        g_in[None],
        g_b_in[None],
        g_fc2[None],
        g_out_bias,
    )


def solution(mesh):
    placed = (
        P("pipe", "dp", "tensor", None),
        P("dp", None),
        P("pipe", None, None),
        P("pipe", None, None),
        P("pipe", None, "tensor"),
        P("pipe", "tensor"),
        P("pipe", "tensor", None),
        P("pipe", None, "tensor"),
        P("pipe", "tensor"),
        P("pipe", "tensor", None),
        P("pipe", None, None),
    )
    return jax.shard_map(
        body,
        mesh=mesh,
        in_specs=placed,
        out_specs=(
            P("pipe", "dp", "tensor", None),
            P("pipe", None, ("tensor", "dp")),
            P("pipe", None, ("tensor", "dp")),
            P("pipe", "dp", "tensor"),
            P("pipe", ("tensor", "dp")),
            P("pipe", ("tensor", "dp"), None),
            P("pipe", "dp", "tensor"),
            P("pipe", ("tensor", "dp")),
            P("pipe", ("tensor", "dp"), None),
            P("pipe", None, ("tensor", "dp")),
        ),
        check_vma=False,
    )
```
